256 devices in a mesh: ctx: 32 (over y, z), head: 8 (over x, core).
Axes of the slice: x: 4, y: 4, z: 8, core: 2. Of those that a mesh axis runs over, the one named last changes fastest.
Arguments:
- queries: bfloat16 [4096, 4096], P('ctx', 'head'), may hold values from -0.75 to 0.75
- keys: bfloat16 [4096, 4096], P('ctx', 'head'), may hold values from -0.75 to 0.75
- values: bfloat16 [4096, 4096], P('ctx', 'head'), may hold values from -0.75 to 0.75
- out_grad: bfloat16 [4096, 4096], P('ctx', 'head'), may hold values from -0.75 to 0.75
- log_decay: float32 [32, 4096], P('head', 'ctx'), may hold values from -1.5 to 0, as said below
- prefix_state: float32 [32, 128, 128], P('head'), may hold values from -3 to 3
- moe_input: bfloat16 [4096, 3072], P('ctx', 'head'), may hold values from -6 to 6
- moe_grad: bfloat16 [4096, 3072], P('ctx', 'head'), may hold values from -6 to 6
- expert_gate: bfloat16 [32, 3072, 4608], P('ctx', None, 'head'), may hold values from -0.109375 to 0.109375
- expert_up: bfloat16 [32, 3072, 4608], P('ctx', None, 'head'), may hold values from -0.109375 to 0.109375
- expert_down: bfloat16 [32, 4608, 3072], P('ctx', 'head'), may hold values from -0.09375 to 0.09375
- expert_ids: int32 [4096, 2], P('ctx'), may hold values from 0 to 31, all different within a row; in each aligned block of 128 rows (0 to 127, 128 to 255, ...) at most 16 rows name the same one
- route_probs: float32 [4096, 2], P('ctx'), may hold values from 0.1 to 1
Outputs:
- query_grad: bfloat16 [4096, 4096], P('ctx', 'head')
- key_grad: bfloat16 [4096, 4096], P('ctx', 'head')
- value_grad: bfloat16 [4096, 4096], P('ctx', 'head')
- moe_input_grad: bfloat16 [4096, 3072], P('ctx', 'head')
The draws below stay inside these ranges and needn't reach their ends.
Inputs may be any that keep to these rules, and one draw needn't show every extreme that they name: `expert_ids`: each row names two different experts. In each block of 128 rows (one ctx index) no expert is named by more than 16 rows, and in every draw some expert is named by exactly 16 rows of some block. `log_decay`: log of the factor by which a head's state is multiplied at a position.
All inputs are finite; a program needn't handle non-finite values.
Results may differ from the reference program's by a relative error of at most 0.019.
Values may be sent and summed in bfloat16 or wider, within the bound.
A program may use at most 128 MiB of HBM per device.

```python
import math
import jax
import jax.numpy as jnp
import numpy as np
from jax import lax

D = 3072
FF = 4608
HEAD_COUNT = 32
HDIM = 128
TOK_DEV = 128
WINDOW_TOKENS = 4096
EXPERTS = 32
CAP = 16
N_CTX = 32
N_HEAD = 8


def draw_log_decay(key, part):
    random_keys_split = jax.random.split(jax.random.fold_in(key, 11), 6)
    fast_share = 0.5
    is_fast = jax.random.uniform(random_keys_split[0], (HEAD_COUNT,)) < fast_share
    fast_rate = jax.random.uniform(random_keys_split[1], (HEAD_COUNT,), minval=1.0 / 50.0, maxval=1.0 / 30.0)
    base_rate = jnp.where(is_fast, fast_rate, 0.3 / WINDOW_TOKENS)
    blocks = WINDOW_TOKENS // TOK_DEV
    block_factor = jnp.exp(jax.random.uniform(random_keys_split[2], (HEAD_COUNT, blocks), minval=-0.6931, maxval=0.6931))
    block_factor = jnp.repeat(block_factor, TOK_DEV, axis=1)
    position_factor = jax.random.uniform(random_keys_split[3], (HEAD_COUNT, WINDOW_TOKENS), minval=0.6, maxval=1.4)
    decay_rate = base_rate[:, None] * block_factor * position_factor
    spike_location = jax.random.randint(random_keys_split[4], (HEAD_COUNT, 2), 0, WINDOW_TOKENS)
    spike_retained = jax.random.uniform(random_keys_split[5], (HEAD_COUNT, 2), minval=0.5, maxval=0.8)
    token_positions = jnp.arange(WINDOW_TOKENS, dtype=jnp.int32)
    spike_events = jnp.sum(jnp.where(token_positions[None, None, :] == spike_location[:, :, None], jnp.log(spike_retained)[:, :, None], 0.0), axis=1)
    return (spike_events - decay_rate).astype(jnp.float32)


def block_levels(own_key, shape, pieces, low, largest):
    factor_of = 1.0
    for dim, blocks in pieces:
        draws = jax.random.uniform(jax.random.fold_in(jax.random.fold_in(own_key, 6), dim), (blocks,), jnp.float32, low / len(pieces), largest / len(pieces))
        factor_of = factor_of * jnp.repeat(jnp.exp(draws), shape[dim] // blocks).reshape((-1,) + (1,) * (len(shape) - 1 - dim))
    return factor_of


def deal_out(key, own, number, rows, count, top, reach, lean):
    order = jax.random.permutation(key, count)
    packed, usual = shares(count, rows * top, reach, lean, True), shares(count, rows * top, reach, lean, False)
    places = jnp.arange(count)

    def named(tallies, turn):
        used = int((tallies > 0).sum())
        fixed = max(1, used // 4)
        moved = fixed + (places - fixed + turn * (used - fixed)) % max(1, count - fixed)
        return jnp.zeros((count,), jnp.int32).at[order[jnp.where(places < fixed, places, moved)]].set(jnp.asarray(tallies, jnp.int32))

    tallies = jnp.where(number % 4 == 0, named(packed, number // 4), named(usual, number - number // 4 - 1))
    mixed = jax.random.permutation(jax.random.fold_in(own, 3), count)
    source_of, receiver = mixed[0:count // 2 * 2:2], mixed[1:count // 2 * 2:2]
    room = jnp.minimum(tallies[source_of] - 1, reach - tallies[receiver]) // 2
    room = jnp.where((source_of == order[0]) | (receiver == order[0]) | (tallies[receiver] == 0), 0, jnp.maximum(room, 0))
    moved = jax.random.randint(jax.random.fold_in(own, 4), (count // 2,), 0, 1 << 20) % (room + 1)
    tallies = tallies.at[source_of].add(-moved).at[receiver].add(moved)
    items = jnp.searchsorted(jnp.cumsum(tallies), jnp.arange(rows * top), side="right").astype(jnp.int32)
    table = items.reshape(top, rows).T
    table = table[jax.random.permutation(jax.random.fold_in(own, 1), rows)]
    turn = jax.random.randint(jax.random.fold_in(own, 2), (rows, 1), 0, top)
    return jnp.take_along_axis(table, (jnp.arange(top)[None, :] + turn) % top, axis=1)


def shares(count, total, bound, slope, full):
    portions = [(1 << 20) // math.isqrt(grade ** slope) + 1 for grade in range(1, count + 1)]
    largest = bound if full else min(bound, max(-(-total // count), total * portions[0] // sum(portions)))
    least = 1 if total - largest >= count - 1 else 0
    holding, surplus = [largest] + [least] * (count - 1), total - largest - least * (count - 1)
    while surplus > 0:
        free = [i for i in range(1, count) if holding[i] < largest] or [i for i in range(1, count) if holding[i] < bound]
        pool, left = sum([portions[i] for i in free]), surplus
        for i in free:
            extra = min(bound - holding[i], max(1, left * portions[i] // pool), surplus)
            holding[i] = holding[i] + extra
            surplus = surplus - extra
    return np.array(holding)


def bell_draw(own_key, shape, width, limit, cuts=(), held_as=jnp.bfloat16):
    values = width * jax.random.normal(own_key, shape, jnp.float32)
    if cuts:
        values = values * block_levels(own_key, shape, cuts, -0.22, 0.18)
    return jnp.clip(values, -limit, limit).astype(held_as)


def setup_inputs(seed: int = 0) -> dict:
    key_of = jax.random.split(jax.random.key(seed), 14)
    queries = bell_draw(key_of[0], (WINDOW_TOKENS, HEAD_COUNT * HDIM), 0.125, 0.75, ((0, 32), (1, 8)))
    keys = bell_draw(key_of[1], (WINDOW_TOKENS, HEAD_COUNT * HDIM), 0.125, 0.75, ((0, 32), (1, 8)))
    values = bell_draw(key_of[2], (WINDOW_TOKENS, HEAD_COUNT * HDIM), 0.125, 0.75, ((0, 32), (1, 8)))
    out_grad = bell_draw(key_of[3], (WINDOW_TOKENS, HEAD_COUNT * HDIM), 0.125, 0.75, ((0, 32), (1, 8)))
    log_decay = draw_log_decay(jax.random.fold_in(key_of[13], 71), 0)
    prefix_state = bell_draw(key_of[5], (HEAD_COUNT, HDIM, HDIM), 0.5, 3.0, ((0, 8),), jnp.float32)
    moe_input = bell_draw(key_of[6], (WINDOW_TOKENS, D), 1.0, 6.0, ((0, 32), (1, 8)))
    moe_grad = bell_draw(key_of[7], (WINDOW_TOKENS, D), 1.0, 6.0, ((0, 32), (1, 8)))
    expert_gate = bell_draw(key_of[8], (EXPERTS, D, FF), D ** -0.5, 0.109375, ((0, 32), (2, 8)))
    expert_up = bell_draw(key_of[9], (EXPERTS, D, FF), D ** -0.5, 0.109375, ((0, 32), (2, 8)))
    expert_down = bell_draw(key_of[10], (EXPERTS, FF, D), FF ** -0.5, 0.09375, ((0, 32), (1, 8)))
    expert_ids_keys = jax.random.split(jax.random.fold_in(key_of[11], 1), WINDOW_TOKENS // TOK_DEV)
    expert_ids_turns = jax.random.permutation(jax.random.fold_in(key_of[11], 3), WINDOW_TOKENS // TOK_DEV)
    expert_ids = jax.vmap(lambda own, number: deal_out(jax.random.fold_in(key_of[11], 2), own, number, TOK_DEV, EXPERTS, 2, CAP, 2))(expert_ids_keys, expert_ids_turns).reshape((WINDOW_TOKENS, 2))
    route_probs = jnp.clip(0.1 + 0.9 * jax.random.uniform(key_of[12], (WINDOW_TOKENS, 2), jnp.float32) ** block_levels(key_of[12], (WINDOW_TOKENS, 2), ((0, 32),), -0.2, 0.2), 0.1, 1.0)
    return dict(queries=queries, keys=keys, values=values, out_grad=out_grad, log_decay=log_decay, prefix_state=prefix_state, moe_input=moe_input, moe_grad=moe_grad, expert_gate=expert_gate, expert_up=expert_up, expert_down=expert_down, expert_ids=expert_ids, route_probs=route_probs)


HIGHEST = lax.Precision.HIGHEST


def decay_factors(log_decay):
    cumulative = jnp.cumsum(log_decay, axis=1)
    totals = cumulative[:, -1]
    token_positions = jnp.arange(log_decay.shape[1], dtype=jnp.int32)
    causal = (token_positions[:, None] >= token_positions[None, :])[None]
    spread = cumulative[:, :, None] - cumulative[:, None, :]
    within = jnp.where(causal, jnp.exp(jnp.where(causal, spread, 0.0)), 0.0)
    tail_decay = jnp.exp(totals[:, None] - cumulative)
    front_decay = jnp.exp(cumulative)
    return totals, within, tail_decay, front_decay


def block_summaries(query_heads, key_heads, value_heads, grad_heads, tail_decay, front_decay):
    key_state = jnp.einsum('hsi,hsj->hij', key_heads * tail_decay[:, :, None], value_heads, precision=HIGHEST)
    query_state = jnp.einsum('hti,htj->hij', query_heads * front_decay[:, :, None], grad_heads, precision=HIGHEST)
    return key_state, query_state


def block_grads(query_heads, key_heads, value_heads, grad_heads, within, tail_decay, front_decay, state_in, state_grad):
    value_scores = jnp.einsum('hti,hsi->hts', grad_heads, value_heads, precision=HIGHEST) * within
    key_scores = jnp.einsum('hti,hsi->hts', query_heads, key_heads, precision=HIGHEST) * within
    query_out = jnp.einsum('hts,hsi->hti', value_scores, key_heads, precision=HIGHEST)
    query_out = query_out + front_decay[:, :, None] * jnp.einsum('htj,hij->hti', grad_heads, state_in, precision=HIGHEST)
    key_out = jnp.einsum('hts,hti->hsi', value_scores, query_heads, precision=HIGHEST)
    key_out = key_out + tail_decay[:, :, None] * jnp.einsum('hsj,hij->hsi', value_heads, state_grad, precision=HIGHEST)
    value_out = jnp.einsum('hts,htj->hsj', key_scores, grad_heads, precision=HIGHEST)
    value_out = value_out + tail_decay[:, :, None] * jnp.einsum('hsi,hij->hsj', key_heads, state_grad, precision=HIGHEST)
    return query_out, key_out, value_out


def swiglu_grads(gate_pre, up_pre, hidden_grad):
    sigmoid = jax.nn.sigmoid(gate_pre)
    gate_grad = hidden_grad * up_pre * sigmoid * (1.0 + gate_pre * (1.0 - sigmoid))
    up_grad = hidden_grad * gate_pre * sigmoid
    return gate_grad.astype(jnp.bfloat16), up_grad.astype(jnp.bfloat16)


def block_slots(block_ids, experts, capacity):
    flat_ids = block_ids.reshape(-1)
    onehot = (flat_ids[:, None] == jnp.arange(experts, dtype=jnp.int32)[None, :]).astype(jnp.int32)
    earlier = jnp.cumsum(onehot, axis=0) - onehot
    slot_rank = jnp.sum(earlier * onehot, axis=1).astype(jnp.int32)
    placed = (flat_ids * capacity + slot_rank).astype(jnp.int32)
    pair_index = jnp.arange(flat_ids.shape[0], dtype=jnp.int32)
    source = jnp.zeros((experts * capacity,), jnp.int32).at[placed].set(pair_index // 2)
    filled = jnp.zeros((experts * capacity,), jnp.float32).at[placed].set(1.0)
    return placed, source, filled


def split_heads(array):
    return array.astype(jnp.float32).reshape(N_CTX, TOK_DEV, HEAD_COUNT, HDIM).transpose(0, 2, 1, 3)


def join_heads(array):
    return array.transpose(0, 2, 1, 3).reshape(WINDOW_TOKENS, HEAD_COUNT * HDIM).astype(jnp.bfloat16)


def reference(queries, keys, values, out_grad, log_decay, prefix_state, moe_input, moe_grad, expert_gate, expert_up, expert_down, expert_ids, route_probs):
    query_blocks = split_heads(queries)
    key_blocks = split_heads(keys)
    value_blocks = split_heads(values)
    grad_blocks = split_heads(out_grad)
    decay_blocks = log_decay.reshape(HEAD_COUNT, N_CTX, TOK_DEV).transpose(1, 0, 2)

    def summarize(items):
        query_heads, key_heads, value_heads, grad_heads, decays = items
        totals, within, tail_decay, front_decay = decay_factors(decays)
        key_state, query_state = block_summaries(query_heads, key_heads, value_heads, grad_heads, tail_decay, front_decay)
        return totals, key_state, query_state

    totals, key_states, query_states = lax.map(summarize, (query_blocks, key_blocks, value_blocks, grad_blocks, decay_blocks))

    def forward(carried, items):
        block_total, key_state = items
        return jnp.exp(block_total)[:, None, None] * carried + key_state, carried

    final_state, states_in = lax.scan(forward, prefix_state, (totals, key_states))

    def backward(carried, items):
        block_total, query_state = items
        return query_state + jnp.exp(block_total)[:, None, None] * carried, carried

    first_grad, states_grad = lax.scan(backward, jnp.zeros_like(prefix_state), (totals, query_states), reverse=True)

    def finish(items):
        query_heads, key_heads, value_heads, grad_heads, decays, state_in, state_grad = items
        block_total, within, tail_decay, front_decay = decay_factors(decays)
        return block_grads(query_heads, key_heads, value_heads, grad_heads, within, tail_decay, front_decay, state_in, state_grad)

    query_out, key_out, value_out = lax.map(finish, (query_blocks, key_blocks, value_blocks, grad_blocks, decay_blocks, states_in, states_grad))

    experts = N_CTX
    capacity = CAP
    placed, source, filled = jax.vmap(lambda block_ids: block_slots(block_ids, experts, capacity))(expert_ids.reshape(N_CTX, TOK_DEV, 2))
    global_source = source + (jnp.arange(N_CTX, dtype=jnp.int32) * TOK_DEV)[:, None]
    rows_source = global_source.reshape(N_CTX, experts, capacity).transpose(1, 0, 2).reshape(experts, N_CTX * capacity)
    rows_filled = filled.reshape(N_CTX, experts, capacity).transpose(1, 0, 2).reshape(experts, N_CTX * capacity)
    span = FF // N_HEAD

    def one_expert(items):
        index, present, gate_w, up_w, down_w = items
        rows_in = (moe_input[index].astype(jnp.float32) * present[:, None]).astype(jnp.bfloat16)
        rows_grad = (moe_grad[index].astype(jnp.float32) * present[:, None]).astype(jnp.bfloat16)
        gate_pre = jnp.dot(rows_in, gate_w, preferred_element_type=jnp.float32)
        up_pre = jnp.dot(rows_in, up_w, preferred_element_type=jnp.float32)
        hidden_grad = jnp.dot(rows_grad, down_w.T, preferred_element_type=jnp.float32)
        gate_grad, up_grad = swiglu_grads(gate_pre, up_pre, hidden_grad)
        gate_parts = gate_grad.astype(jnp.float32).reshape(-1, N_HEAD, span)
        up_parts = up_grad.astype(jnp.float32).reshape(-1, N_HEAD, span)
        parts = jnp.einsum('nhf,dhf->hnd', gate_parts, gate_w.astype(jnp.float32).reshape(D, N_HEAD, span))
        parts = parts + jnp.einsum('nhf,dhf->hnd', up_parts, up_w.astype(jnp.float32).reshape(D, N_HEAD, span))
        parts = lax.optimization_barrier(parts.astype(jnp.bfloat16))
        return jnp.sum(parts.astype(jnp.float32), axis=0).astype(jnp.bfloat16)

    expert_back = lax.map(one_expert, (rows_source, rows_filled, expert_gate, expert_up, expert_down))
    table = expert_back.reshape(experts * N_CTX * capacity, D)
    pair_ids = expert_ids.reshape(N_CTX, TOK_DEV * 2)
    slot_rank = placed - pair_ids * capacity
    rows_index = pair_ids * (N_CTX * capacity) + (jnp.arange(N_CTX, dtype=jnp.int32) * capacity)[:, None] + slot_rank
    picked = table[rows_index.reshape(-1)].astype(jnp.float32).reshape(WINDOW_TOKENS, 2, D)
    moe_input_grad = jnp.sum(picked * route_probs[:, :, None], axis=1).astype(jnp.bfloat16)
    return join_heads(query_out), join_heads(key_out), join_heads(value_out), moe_input_grad
```

```python
import functools

import jax
import jax.numpy as jnp
from jax import lax
from jax.experimental import pallas as pl
from jax.experimental.pallas import tpu as pltpu
from jax.sharding import PartitionSpec as P

F32 = jnp.float32
BF16 = jnp.bfloat16
MESH = pl.DeviceIdType.MESH
NX = 4
LANES = 128


def dot(a, b):
    return jnp.dot(a, b, preferred_element_type=F32)


def dot_t(a, b):
    return lax.dot_general(a, b, (((1,), (1,)), ((), ())), preferred_element_type=F32)


def dot_l(a, b):
    return lax.dot_general(a, b, (((0,), (0,)), ((), ())), preferred_element_type=F32)


def pieces(value, count):
    parts = []
    for _ in range(count):
        part = value.astype(BF16)
        parts.append(part)
        value = value - part.astype(F32)
    return parts


def kernel(
    size,
    q_ref, k_ref, v_ref, g_ref, decay_ref, prefix_ref, in_ref, grad_ref, gate_hbm, up_hbm, down_hbm, ids_ref, probs_ref,
    dq_ref, dk_ref, dv_ref, dx_ref,
    gate, up, down, out_rows, rows, acc_gate, acc_up, acc_hidden, part, part_in, total, far_left, far_right, near_left,
    near_right, back, table, weights, state_out, state_all, scan_out, state, local, front_s, tail_s,
    w_sem, one_sem, a2a_recv, ring_recv, sib_recv, send_sem, part_recv, far_recv, near_recv, back_recv,
):
    E, NY, NZ, T, CAP, DC, HL, NG = size
    EG = E // NG
    NR = EG * CAP
    HALF = NR // 2
    W = 2 * DC
    SR = HL * LANES // E
    SHIFT = NZ.bit_length() - 1

    c, h = lax.axis_index("ctx"), lax.axis_index("head")
    x, core = h // 2, h % 2
    y, z = c // NZ, c % NZ
    x_left, x_right, x_far = (x + NX - 1) % NX, (x + 1) % NX, (x + 2) % NX
    right = (c, x_right * 2 + core)
    left = (c, x_left * 2 + core)
    sibling = (c, x * 2 + 1 - core)
    mine = pl.ds(pl.multiple_of(core * DC, LANES), DC)
    other = pl.ds(pl.multiple_of((1 - core) * DC, LANES), DC)

    def forth(d):
        return ((y + d // NZ) % NY) * NZ + (z + d % NZ) % NZ

    def back_to(d):
        return ((y + NY - d // NZ) % NY) * NZ + (z + NZ - d % NZ) % NZ

    def group(g):
        return pl.ds(g * NR, NR)

    def remote(src, dst, send, recv, device):
        return pltpu.make_async_remote_copy(
            src_ref=src, dst_ref=dst, send_sem=send, recv_sem=recv, device_id=device, device_id_type=MESH
        )

    def arrived(ref, recv):
        remote(ref, ref, recv, recv, right).wait_recv()

    def sent(ref, send):
        remote(ref, ref, send, send, right).wait_send()

    barrier = pltpu.get_barrier_semaphore()

    def greet(d, carry):
        pl.semaphore_signal(barrier, inc=1, device_id=(forth(d), h), device_id_type=MESH)
        return carry

    lax.fori_loop(1, E, greet, 0)
    for device in (right, left, sibling):
        pl.semaphore_signal(barrier, inc=1, device_id=device, device_id_type=MESH)

    loads = [
        pltpu.make_async_copy(hbm.at[0], vmem, w_sem.at[i])
        for i, (hbm, vmem) in enumerate(((gate_hbm, gate), (up_hbm, up), (down_hbm, down)))
    ]
    for load in loads:
        load.start()

    lane = lax.broadcasted_iota(jnp.int32, (T, E), 1)
    expert = (((y + (lane >> SHIFT)) & (NY - 1)) << SHIFT) + ((z + (lane & (NZ - 1))) & (NZ - 1))
    first = (ids_ref[:, 0:1] == expert).astype(F32)
    second = (ids_ref[:, 1:2] == expert).astype(F32)
    named = first + second
    t_row = lax.broadcasted_iota(jnp.int32, (T, T), 0)
    t_col = lax.broadcasted_iota(jnp.int32, (T, T), 1)
    earlier = dot((t_row > t_col).astype(F32).astype(BF16), named.astype(BF16))
    slot = jnp.where(named > 0.5, earlier, -1.0).astype(BF16)
    r_row = lax.broadcasted_iota(jnp.int32, (E * CAP, E), 0)
    e_col = lax.broadcasted_iota(jnp.int32, (E * CAP, E), 1)
    spread = (r_row // CAP == e_col).astype(F32).astype(BF16)
    want = (lax.broadcasted_iota(jnp.int32, (E * CAP, T), 0) % CAP).astype(F32)
    pick = (dot_t(spread, slot) == want).astype(F32).astype(BF16)
    out_rows[:, 0] = dot(pick, in_ref[...]).astype(BF16).reshape(E, CAP, DC)
    out_rows[:, 1] = dot(pick, grad_ref[...]).astype(BF16).reshape(E, CAP, DC)

    pl.semaphore_wait(barrier, E - 1 + 3)

    def dispatch(d, carry):
        remote(
            out_rows.at[d], rows.at[:, x, pl.ds(d * CAP, CAP), mine], send_sem.at[0], a2a_recv.at[d // EG], (forth(d), h)
        ).start()
        return carry

    own = pltpu.make_async_copy(out_rows.at[0], rows.at[:, x, pl.ds(0, CAP), mine], one_sem.at[0])
    own.start()
    lax.fori_loop(1, E, dispatch, 0)

    cum = jnp.zeros((HL, T), F32)
    upto = (t_row <= t_col).astype(F32).astype(BF16)
    for piece in pieces(decay_ref[...], 3):
        cum = cum + dot(piece, upto)
    slab = lax.broadcasted_iota(jnp.int32, (LANES, LANES), 0) % SR
    for i in range(HL):
        cols = slice(i * LANES, (i + 1) * LANES)
        along = jnp.broadcast_to(cum[i : i + 1, :], (T, T))
        down_t = along.T
        total_b = jnp.broadcast_to(down_t[T - 1 : T, :], (T, T))
        front_s[i] = jnp.exp(down_t)
        tail_s[i] = jnp.exp(total_b - down_t)
        q, k, v, g = q_ref[:, cols], k_ref[:, cols], v_ref[:, cols], g_ref[:, cols]
        state_out[cols, 0:LANES] = dot_l((k.astype(F32) * tail_s[i]).astype(BF16), v).astype(BF16)
        state_out[cols, LANES : 2 * LANES] = dot_l((q.astype(F32) * front_s[i]).astype(BF16), g).astype(BF16)
        d0, d1, d2 = [piece.astype(F32) for piece in pieces(jnp.exp(total_b), 3)]
        state_out[cols, 2 * LANES :] = jnp.where(slab == 0, d0, jnp.where(slab == 1, d1, d2)).astype(BF16)

    def slices(ref, p):
        return ref.at[pl.ds(pl.multiple_of(p * SR, SR), SR), :]

    def states(d, carry):
        remote(slices(state_out, forth(d)), slices(state_all, c), send_sem.at[1], one_sem.at[1], (forth(d), h)).start()
        return carry

    own_state = pltpu.make_async_copy(slices(state_out, c), slices(state_all, c), one_sem.at[2])
    own_state.start()
    lax.fori_loop(1, E, states, 0)

    for i in range(HL):
        cols = slice(i * LANES, (i + 1) * LANES)
        along = jnp.broadcast_to(cum[i : i + 1, :], (T, T))
        down_t = along.T
        q, k, v, g = q_ref[:, cols], k_ref[:, cols], v_ref[:, cols], g_ref[:, cols]
        low, high = t_row >= t_col, t_row <= t_col
        within = jnp.where(low, jnp.exp(jnp.where(low, down_t - along, 0.0)), 0.0)
        within_t = jnp.where(high, jnp.exp(jnp.where(high, along - down_t, 0.0)), 0.0)
        local[0, :, cols] = dot((dot_t(g, v) * within).astype(BF16), k)
        local[1, :, cols] = dot((dot_t(v, g) * within_t).astype(BF16), q)
        local[2, :, cols] = dot((dot_t(k, q) * within_t).astype(BF16), g)

    chance = first * probs_ref[:, 0:1] + second * probs_ref[:, 1:2]
    pick_t = dot_t(slot, spread) == (lax.broadcasted_iota(jnp.int32, (T, E * CAP), 1) % CAP).astype(F32)
    for i, piece in enumerate(pieces(chance, 3)):
        weights[i] = jnp.where(pick_t, dot_t(piece, spread), 0.0).astype(BF16)

    def scan_states():
        own_state.wait()
        arrived(state_all.at[pl.ds(0, (E - 1) * SR), :], one_sem.at[1])

        def step(reverse, column, i, carried):
            at = E - 1 - i if reverse else i
            tile = slices(state_all, at)[...].astype(F32)
            factor = tile[0:1, 2 * LANES :] + tile[1:2, 2 * LANES :] + tile[2:3, 2 * LANES :]
            columns = slice(column * LANES, (column + 1) * LANES)
            slices(scan_out, at)[:, columns] = carried.astype(BF16)
            return factor * carried + tile[:, columns]

        lax.fori_loop(0, E, functools.partial(step, False, 0), slices(prefix_ref, c)[...])
        lax.fori_loop(0, E, functools.partial(step, True, 1), jnp.zeros((SR, LANES), F32))

        def give(d, carry):
            remote(slices(scan_out, forth(d)), slices(state, c), send_sem.at[2], one_sem.at[3], (forth(d), h)).start()
            return carry

        own_scan.start()
        lax.fori_loop(1, E, give, 0)

    own_scan = pltpu.make_async_copy(slices(scan_out, c), slices(state, c), one_sem.at[4])

    def finish_states():
        own_scan.wait()
        arrived(state.at[pl.ds(0, (E - 1) * SR), :], one_sem.at[3])
        for i in range(HL):
            cols = slice(i * LANES, (i + 1) * LANES)
            k, v, g = k_ref[:, cols], v_ref[:, cols], g_ref[:, cols]
            s_in, s_grad = state[cols, 0:LANES], state[cols, LANES : 2 * LANES]
            dq_ref[:, cols] = (local[0, :, cols] + front_s[i] * dot_t(g, s_in)).astype(BF16)
            dk_ref[:, cols] = (local[1, :, cols] + tail_s[i] * dot_t(v, s_grad)).astype(BF16)
            dv_ref[:, cols] = (local[2, :, cols] + tail_s[i] * dot(k, s_grad)).astype(BF16)

    def to_sibling(ref, which, send):
        remote(ref, ref, send_sem.at[send], sib_recv.at[which], sibling).start()

    def gather_1(g):
        if g == 0:
            own.wait()
        lead = CAP if g == 0 else 0
        arrived(rows.at[:, x, pl.ds(g * NR + lead, NR - lead), mine], a2a_recv.at[g])
        ref = rows.at[:, x, group(g), mine]
        remote(ref, ref, send_sem.at[3], ring_recv.at[g, 0], right).start()
        remote(ref, ref, send_sem.at[4], ring_recv.at[g, 1], left).start()
        to_sibling(ref, (g, 0), 7)

    def gather_2(g):
        from_left, from_right = rows.at[:, x_left, group(g), mine], rows.at[:, x_right, group(g), mine]
        arrived(from_left, ring_recv.at[g, 0])
        ref = rows.at[0, x_left, group(g), mine]
        remote(ref, ref, send_sem.at[5], ring_recv.at[g, 2], right).start()
        to_sibling(from_left, (g, 1), 8)
        arrived(from_right, ring_recv.at[g, 1])
        ref = rows.at[1, x_right, group(g), mine]
        remote(ref, ref, send_sem.at[6], ring_recv.at[g, 3], left).start()
        to_sibling(from_right, (g, 2), 9)

    def gather_3(g):
        for i in range(2):
            ref = rows.at[i, x_far, group(g), mine]
            arrived(ref, ring_recv.at[g, 2 + i])
            to_sibling(ref, (g, 3 + i), 10 + i)

    def expert(g):
        for i, at in enumerate((x, x_left, x_right, x_far)):
            if i < 3:
                arrived(rows.at[:, at, group(g), other], sib_recv.at[g, i])
            else:
                arrived(rows.at[0, at, group(g), other], sib_recv.at[g, 3])
                arrived(rows.at[1, at, group(g), other], sib_recv.at[g, 4])
            deep = pl.ds(pl.multiple_of(at * W, LANES), W)
            r_in, r_grad = rows[0, at, group(g), :], rows[1, at, group(g), :]
            for acc, value in (
                (acc_gate, dot(r_in, gate[deep, :])),
                (acc_up, dot(r_in, up[deep, :])),
                (acc_hidden, dot_t(r_grad, down[:, deep])),
            ):
                acc[...] = value if i == 0 else acc[...] + value
        gate_pre, up_pre, hidden = acc_gate[...], acc_up[...], acc_hidden[...]
        sig = 1.0 / (1.0 + jnp.exp(-gate_pre))
        gate_grad = (hidden * up_pre * sig * (1.0 + gate_pre * (1.0 - sig))).astype(BF16)
        up_grad = (hidden * gate_pre * sig).astype(BF16)

        def column(i, carry):
            deep = pl.ds(pl.multiple_of(i * W, LANES), W)
            part[i, group(g), :] = (dot_t(gate_grad, gate[deep, :]) + dot_t(up_grad, up[deep, :])).astype(BF16)
            return carry

        lax.fori_loop(0, NX, column, 0)

    def reduce_1(g):
        remote(
            part.at[:, group(g), other], part_in.at[:, group(g), :], send_sem.at[12], part_recv.at[g], sibling
        ).start()

    def pair_sum(at, span):
        return part[at, span, mine].astype(F32) + part_in[at, span, :].astype(F32)

    def reduce_2(g):
        arrived(part_in.at[:, group(g), :], part_recv.at[g])
        total[0, group(g), :] = pair_sum(x_far, group(g)).astype(BF16)
        remote(
            total.at[0, pl.ds(g * NR, HALF), :], far_left.at[pl.ds(g * HALF, HALF), :], send_sem.at[13], far_recv.at[g, 0], right
        ).start()
        remote(
            total.at[0, pl.ds(g * NR + HALF, HALF), :], far_right.at[pl.ds(g * HALF, HALF), :], send_sem.at[14], far_recv.at[g, 1], left
        ).start()

    def reduce_3(g):
        half = pl.ds(g * HALF, HALF)
        lower, upper = pl.ds(g * NR, HALF), pl.ds(g * NR + HALF, HALF)
        arrived(far_left.at[half, :], far_recv.at[g, 0])
        total[1, lower, :] = (pair_sum(x_right, lower) + far_left[half, :].astype(F32)).astype(BF16)
        total[1, upper, :] = pair_sum(x_right, upper).astype(BF16)
        remote(
            total.at[1, group(g), :], near_left.at[group(g), :], send_sem.at[15], near_recv.at[g, 0], right
        ).start()
        arrived(far_right.at[half, :], far_recv.at[g, 1])
        total[2, lower, :] = pair_sum(x_left, lower).astype(BF16)
        total[2, upper, :] = (pair_sum(x_left, upper) + far_right[half, :].astype(F32)).astype(BF16)
        remote(
            total.at[2, group(g), :], near_right.at[group(g), :], send_sem.at[16], near_recv.at[g, 1], left
        ).start()

    def slots(ref, d):
        return ref.at[pl.ds(pl.multiple_of(d * CAP, CAP), CAP), :]

    own_back = pltpu.make_async_copy(slots(back, 0), slots(table, 0), one_sem.at[5])

    def reduce_4(g):
        arrived(near_left.at[group(g), :], near_recv.at[g, 0])
        arrived(near_right.at[group(g), :], near_recv.at[g, 1])
        value = near_left[group(g), :].astype(F32) + near_right[group(g), :].astype(F32)
        back[group(g), :] = (pair_sum(x, group(g)) + value).astype(BF16)

        def give(d, carry):
            remote(slots(back, d), slots(table, d), send_sem.at[17], back_recv.at[0], (back_to(d), h)).start()
            return carry

        if g == 0:
            own_back.start()
        lax.fori_loop(max(g * EG, 1), (g + 1) * EG, give, 0)

    for load in loads:
        load.wait()
    for i in range(NG + 5):
        for ahead, stage in enumerate((gather_1, gather_2, gather_3)):
            if 0 <= i - ahead < NG:
                stage(i - ahead)
        if i == NG - 1:
            scan_states()
        if 0 <= i - 2 < NG:
            expert(i - 2)
            reduce_1(i - 2)
        if i == NG + 1:
            finish_states()
        for ahead, stage in ((3, reduce_2), (4, reduce_3), (5, reduce_4)):
            if 0 <= i - ahead < NG:
                stage(i - ahead)

    own_back.wait()
    arrived(table.at[pl.ds(0, (E - 1) * CAP), :], back_recv.at[0])
    found = table[...]
    dx_ref[...] = (dot(weights[0], found) + dot(weights[1], found) + dot(weights[2], found)).astype(BF16)

    ring, half_ring = rows.at[:, 0, :, 0:DC], rows.at[0, 0, :, 0:DC]
    for i, ref in (
        (0, out_rows.at[pl.ds(1, E - 1)]),
        (1, state_out.at[pl.ds(0, (E - 1) * SR), :]),
        (2, scan_out.at[pl.ds(0, (E - 1) * SR), :]),
        (3, ring), (4, ring), (5, half_ring), (6, half_ring),
        (7, ring), (8, ring), (9, ring), (10, half_ring), (11, half_ring),
        (12, part_in), (13, far_left), (14, far_right), (15, near_left), (16, near_right),
        (17, back.at[pl.ds(0, (E - 1) * CAP), :]),
    ):
        sent(ref, send_sem.at[i])


def solution(mesh):
    E = mesh.shape["ctx"]
    NZ = min(8, E // 2)

    def shards(queries, keys, values, out_grad, log_decay, prefix_state, moe_input, moe_grad, gate, up, down, ids, probs):
        T, HL = queries.shape[0], log_decay.shape[0]
        DC, D, FL = moe_input.shape[1], gate.shape[1], gate.shape[2]
        CAP = 4 * T // E
        NG = min(4, E // 2)
        ROWS, NR = E * CAP, E * CAP // NG
        vmem = pl.BlockSpec(memory_space=pltpu.VMEM)
        hbm = pl.BlockSpec(memory_space=pl.ANY)
        size = (E, E // NZ, NZ, T, CAP, DC, HL, NG)
        dma = pltpu.SemaphoreType.DMA
        return pl.pallas_call(
            functools.partial(kernel, size),
            out_shape=[jax.ShapeDtypeStruct((T, HL * LANES), BF16)] * 3 + [jax.ShapeDtypeStruct((T, DC), BF16)],
            in_specs=[vmem] * 8 + [hbm] * 3 + [vmem] * 2,
            out_specs=[vmem] * 4,
            scratch_shapes=[
                pltpu.VMEM((D, FL), BF16),
                pltpu.VMEM((D, FL), BF16),
                pltpu.VMEM((FL, D), BF16),
                pltpu.VMEM((E, 2, CAP, DC), BF16),
                pltpu.VMEM((2, NX, ROWS, 2 * DC), BF16),
                pltpu.VMEM((NR, FL), F32),
                pltpu.VMEM((NR, FL), F32),
                pltpu.VMEM((NR, FL), F32),
                pltpu.VMEM((NX, ROWS, 2 * DC), BF16),
                pltpu.VMEM((NX, ROWS, DC), BF16),
                pltpu.VMEM((3, ROWS, DC), BF16),
                pltpu.VMEM((ROWS // 2, DC), BF16),
                pltpu.VMEM((ROWS // 2, DC), BF16),
                pltpu.VMEM((ROWS, DC), BF16),
                pltpu.VMEM((ROWS, DC), BF16),
                pltpu.VMEM((ROWS, DC), BF16),
                pltpu.VMEM((ROWS, DC), BF16),
                pltpu.VMEM((3, T, ROWS), BF16),
                pltpu.VMEM((HL * LANES, 3 * LANES), BF16),
                pltpu.VMEM((HL * LANES, 3 * LANES), BF16),
                pltpu.VMEM((HL * LANES, 2 * LANES), BF16),
                pltpu.VMEM((HL * LANES, 2 * LANES), BF16),
                pltpu.VMEM((3, T, HL * LANES), F32),
                pltpu.VMEM((HL, T, LANES), F32),
                pltpu.VMEM((HL, T, LANES), F32),
                dma((3,)),
                dma((6,)),
                dma((NG,)),
                dma((NG, 4)),
                dma((NG, 5)),
                dma((18,)),
                dma((NG,)),
                dma((NG, 2)),
                dma((NG, 2)),
                dma((1,)),
            ],
            compiler_params=pltpu.CompilerParams(
                collective_id=0, has_side_effects=True, vmem_limit_bytes=52 * 1024 * 1024
            ),
        )(
            queries, keys, values, out_grad, log_decay, prefix_state.reshape(HL * LANES, LANES),
            moe_input, moe_grad, gate, up, down, ids, probs,
        )

    in_specs = (
        P("ctx", "head"),
        P("ctx", "head"),
        P("ctx", "head"),
        P("ctx", "head"),
        P("head", "ctx"),
        P("head", None, None),
        P("ctx", "head"),
        P("ctx", "head"),
        P("ctx", None, "head"),
        P("ctx", None, "head"),
        P("ctx", "head", None),
        P("ctx", None),
        P("ctx", None),
    )
    out_specs = (P("ctx", "head"), P("ctx", "head"), P("ctx", "head"), P("ctx", "head"))
    return jax.shard_map(shards, mesh=mesh, in_specs=in_specs, out_specs=out_specs, check_vma=False)
```

```python
import functools

import jax
import jax.numpy as jnp
from jax import lax
from jax.experimental import pallas as pl
from jax.experimental.pallas import tpu as pltpu
from jax.sharding import PartitionSpec as P

F32 = jnp.float32
BF16 = jnp.bfloat16
MESH = pl.DeviceIdType.MESH
NX = 4
LANES = 128


def dot(a, b):
    return jnp.dot(a, b, preferred_element_type=F32)


def dot_t(a, b):
    return lax.dot_general(a, b, (((1,), (1,)), ((), ())), preferred_element_type=F32)


def dot_l(a, b):
    return lax.dot_general(a, b, (((0,), (0,)), ((), ())), preferred_element_type=F32)


def pieces(value, count):
    parts = []
    for _ in range(count):
        part = value.astype(BF16)
        parts.append(part)
        value = value - part.astype(F32)
    return parts


def kernel(
    size,
    q_ref, k_ref, v_ref, g_ref, decay_ref, prefix_ref, in_ref, grad_ref, gate_hbm, up_hbm, down_hbm, ids_ref, probs_ref,
    dq_ref, dk_ref, dv_ref, dx_ref,
    gate, up, down, out_rows, rows, acc_gate, acc_up, acc_hidden, part, part_in, total, far_left, far_right, near_left,
    near_right, back, table, weights, state_out, state_all, scan_out, state, local, front_s, tail_s,
    w_sem, one_sem, a2a_recv, ring_recv, sib_recv, send_sem, part_recv, far_recv, near_recv, back_recv,
):
    E, NY, NZ, T, CAP, DC, HL, NG = size
    EG = E // NG
    NR = EG * CAP
    HALF = NR // 2
    W = 2 * DC
    SR = HL * LANES // E
    SHIFT = NZ.bit_length() - 1

    c, h = lax.axis_index("ctx"), lax.axis_index("head")
    x, core = h // 2, h % 2
    y, z = c // NZ, c % NZ
    x_left, x_right, x_far = (x + NX - 1) % NX, (x + 1) % NX, (x + 2) % NX
    right = (c, x_right * 2 + core)
    left = (c, x_left * 2 + core)
    sibling = (c, x * 2 + 1 - core)
    mine = pl.ds(pl.multiple_of(core * DC, LANES), DC)
    other = pl.ds(pl.multiple_of((1 - core) * DC, LANES), DC)

    def forth(d):
        return ((y + d // NZ) % NY) * NZ + (z + d % NZ) % NZ

    def back_to(d):
        return ((y + NY - d // NZ) % NY) * NZ + (z + NZ - d % NZ) % NZ

    def group(g):
        return pl.ds(g * NR, NR)

    def remote(src, dst, send, recv, device):
        return pltpu.make_async_remote_copy(
            src_ref=src, dst_ref=dst, send_sem=send, recv_sem=recv, device_id=device, device_id_type=MESH
        )

    def arrived(ref, recv):
        remote(ref, ref, recv, recv, right).wait_recv()

    def sent(ref, send):
        remote(ref, ref, send, send, right).wait_send()

    barrier = pltpu.get_barrier_semaphore()

    def greet(d, carry):
        pl.semaphore_signal(barrier, inc=1, device_id=(forth(d), h), device_id_type=MESH)
        return carry

    lax.fori_loop(1, E, greet, 0)
    for device in (right, left, sibling):
        pl.semaphore_signal(barrier, inc=1, device_id=device, device_id_type=MESH)

    loads = [
        pltpu.make_async_copy(hbm.at[0], vmem, w_sem.at[i])
        for i, (hbm, vmem) in enumerate(((gate_hbm, gate), (up_hbm, up), (down_hbm, down)))
    ]
    for load in loads:
        load.start()

    ahead = lax.broadcasted_iota(jnp.int32, (E, T), 0)
    expert = (((y + (ahead >> SHIFT)) & (NY - 1)) << SHIFT) + ((z + (ahead & (NZ - 1))) & (NZ - 1))
    first = (ids_ref[0:1, :] == expert).astype(F32)
    second = (ids_ref[1:2, :] == expert).astype(F32)
    named = first + second
    t_row = lax.broadcasted_iota(jnp.int32, (T, T), 0)
    t_col = lax.broadcasted_iota(jnp.int32, (T, T), 1)
    earlier = dot(named.astype(BF16), (t_row < t_col).astype(F32).astype(BF16))
    slot = jnp.where(named > 0.5, earlier, -1.0).astype(BF16)
    r_row = lax.broadcasted_iota(jnp.int32, (E * CAP, E), 0)
    e_col = lax.broadcasted_iota(jnp.int32, (E * CAP, E), 1)
    spread = (r_row // CAP == e_col).astype(F32).astype(BF16)
    want = (lax.broadcasted_iota(jnp.int32, (E * CAP, T), 0) % CAP).astype(F32)
    pick = (dot(spread, slot) == want).astype(F32).astype(BF16)
    out_rows[:, 0] = dot(pick, in_ref[...]).astype(BF16).reshape(E, CAP, DC)
    out_rows[:, 1] = dot(pick, grad_ref[...]).astype(BF16).reshape(E, CAP, DC)

    pl.semaphore_wait(barrier, E - 1 + 3)

    def dispatch(d, carry):
        remote(
            out_rows.at[d], rows.at[:, x, pl.ds(d * CAP, CAP), mine], send_sem.at[0], a2a_recv.at[d // EG], (forth(d), h)
        ).start()
        return carry

    own = pltpu.make_async_copy(out_rows.at[0], rows.at[:, x, pl.ds(0, CAP), mine], one_sem.at[0])
    own.start()
    lax.fori_loop(1, E, dispatch, 0)

    cum = jnp.zeros((HL, T), F32)
    upto = (t_row <= t_col).astype(F32).astype(BF16)
    for piece in pieces(decay_ref[...], 3):
        cum = cum + dot(piece, upto)
    slab = lax.broadcasted_iota(jnp.int32, (LANES, LANES), 0) % SR
    for i in range(HL):
        cols = slice(i * LANES, (i + 1) * LANES)
        along = jnp.broadcast_to(cum[i : i + 1, :], (T, T))
        down_t = along.T
        total_b = jnp.broadcast_to(down_t[T - 1 : T, :], (T, T))
        front_s[i] = jnp.exp(down_t)
        tail_s[i] = jnp.exp(total_b - down_t)
        q, k, v, g = q_ref[:, cols], k_ref[:, cols], v_ref[:, cols], g_ref[:, cols]
        state_out[cols, 0:LANES] = dot_l((k.astype(F32) * tail_s[i]).astype(BF16), v).astype(BF16)
        state_out[cols, LANES : 2 * LANES] = dot_l((q.astype(F32) * front_s[i]).astype(BF16), g).astype(BF16)
        d0, d1, d2 = [piece.astype(F32) for piece in pieces(jnp.exp(total_b), 3)]
        state_out[cols, 2 * LANES :] = jnp.where(slab == 0, d0, jnp.where(slab == 1, d1, d2)).astype(BF16)

    def slices(ref, p):
        return ref.at[pl.ds(pl.multiple_of(p * SR, SR), SR), :]

    def states(d, carry):
        remote(slices(state_out, forth(d)), slices(state_all, c), send_sem.at[1], one_sem.at[1], (forth(d), h)).start()
        return carry

    own_state = pltpu.make_async_copy(slices(state_out, c), slices(state_all, c), one_sem.at[2])
    own_state.start()
    lax.fori_loop(1, E, states, 0)

    for i in range(HL):
        cols = slice(i * LANES, (i + 1) * LANES)
        along = jnp.broadcast_to(cum[i : i + 1, :], (T, T))
        down_t = along.T
        q, k, v, g = q_ref[:, cols], k_ref[:, cols], v_ref[:, cols], g_ref[:, cols]
        low, high = t_row >= t_col, t_row <= t_col
        within = jnp.where(low, jnp.exp(jnp.where(low, down_t - along, 0.0)), 0.0)
        within_t = jnp.where(high, jnp.exp(jnp.where(high, along - down_t, 0.0)), 0.0)
        local[0, :, cols] = dot((dot_t(g, v) * within).astype(BF16), k)
        local[1, :, cols] = dot((dot_t(v, g) * within_t).astype(BF16), q)
        local[2, :, cols] = dot((dot_t(k, q) * within_t).astype(BF16), g)

    chance = first * probs_ref[0:1, :] + second * probs_ref[1:2, :]
    r_col = lax.broadcasted_iota(jnp.int32, (E, E * CAP), 1)
    spread_t = (r_col // CAP == lax.broadcasted_iota(jnp.int32, (E, E * CAP), 0)).astype(F32).astype(BF16)
    pick_t = dot_l(slot, spread_t) == (lax.broadcasted_iota(jnp.int32, (T, E * CAP), 1) % CAP).astype(F32)
    for i, piece in enumerate(pieces(chance, 3)):
        weights[i] = jnp.where(pick_t, dot_l(piece, spread_t), 0.0).astype(BF16)

    def scan_states():
        own_state.wait()
        arrived(state_all.at[pl.ds(0, (E - 1) * SR), :], one_sem.at[1])

        def step(reverse, column, i, carried):
            at = E - 1 - i if reverse else i
            tile = slices(state_all, at)[...].astype(F32)
            factor = tile[0:1, 2 * LANES :] + tile[1:2, 2 * LANES :] + tile[2:3, 2 * LANES :]
            columns = slice(column * LANES, (column + 1) * LANES)
            slices(scan_out, at)[:, columns] = carried.astype(BF16)
            return factor * carried + tile[:, columns]

        lax.fori_loop(0, E, functools.partial(step, False, 0), slices(prefix_ref, c)[...])
        lax.fori_loop(0, E, functools.partial(step, True, 1), jnp.zeros((SR, LANES), F32))

        def give(d, carry):
            remote(slices(scan_out, forth(d)), slices(state, c), send_sem.at[2], one_sem.at[3], (forth(d), h)).start()
            return carry

        own_scan.start()
        lax.fori_loop(1, E, give, 0)

    own_scan = pltpu.make_async_copy(slices(scan_out, c), slices(state, c), one_sem.at[4])

    def finish_states():
        own_scan.wait()
        arrived(state.at[pl.ds(0, (E - 1) * SR), :], one_sem.at[3])
        for i in range(HL):
            cols = slice(i * LANES, (i + 1) * LANES)
            k, v, g = k_ref[:, cols], v_ref[:, cols], g_ref[:, cols]
            s_in, s_grad = state[cols, 0:LANES], state[cols, LANES : 2 * LANES]
            dq_ref[:, cols] = (local[0, :, cols] + front_s[i] * dot_t(g, s_in)).astype(BF16)
            dk_ref[:, cols] = (local[1, :, cols] + tail_s[i] * dot_t(v, s_grad)).astype(BF16)
            dv_ref[:, cols] = (local[2, :, cols] + tail_s[i] * dot(k, s_grad)).astype(BF16)

    def to_sibling(ref, which, send):
        remote(ref, ref, send_sem.at[send], sib_recv.at[which], sibling).start()

    def gather_1(g):
        if g == 0:
            own.wait()
        lead = CAP if g == 0 else 0
        arrived(rows.at[:, x, pl.ds(g * NR + lead, NR - lead), mine], a2a_recv.at[g])
        ref = rows.at[:, x, group(g), mine]
        remote(ref, ref, send_sem.at[3], ring_recv.at[g, 0], right).start()
        remote(ref, ref, send_sem.at[4], ring_recv.at[g, 1], left).start()
        to_sibling(ref, (g, 0), 7)

    def gather_2(g):
        from_left, from_right = rows.at[:, x_left, group(g), mine], rows.at[:, x_right, group(g), mine]
        arrived(from_left, ring_recv.at[g, 0])
        ref = rows.at[0, x_left, group(g), mine]
        remote(ref, ref, send_sem.at[5], ring_recv.at[g, 2], right).start()
        to_sibling(from_left, (g, 1), 8)
        arrived(from_right, ring_recv.at[g, 1])
        ref = rows.at[1, x_right, group(g), mine]
        remote(ref, ref, send_sem.at[6], ring_recv.at[g, 3], left).start()
        to_sibling(from_right, (g, 2), 9)

    def gather_3(g):
        for i in range(2):
            ref = rows.at[i, x_far, group(g), mine]
            arrived(ref, ring_recv.at[g, 2 + i])
            to_sibling(ref, (g, 3 + i), 10 + i)

    def expert(g):
        for i, at in enumerate((x, x_left, x_right, x_far)):
            if i < 3:
                arrived(rows.at[:, at, group(g), other], sib_recv.at[g, i])
            else:
                arrived(rows.at[0, at, group(g), other], sib_recv.at[g, 3])
                arrived(rows.at[1, at, group(g), other], sib_recv.at[g, 4])
            deep = pl.ds(pl.multiple_of(at * W, LANES), W)
            r_in, r_grad = rows[0, at, group(g), :], rows[1, at, group(g), :]
            for acc, value in (
                (acc_gate, dot_t(r_in, gate[:, deep])),
                (acc_up, dot_t(r_in, up[:, deep])),
                (acc_hidden, dot_t(r_grad, down[:, deep])),
            ):
                acc[...] = value if i == 0 else acc[...] + value
        gate_pre, up_pre, hidden = acc_gate[...], acc_up[...], acc_hidden[...]
        sig = 1.0 / (1.0 + jnp.exp(-gate_pre))
        gate_grad = (hidden * up_pre * sig * (1.0 + gate_pre * (1.0 - sig))).astype(BF16)
        up_grad = (hidden * gate_pre * sig).astype(BF16)

        def column(i, carry):
            deep = pl.ds(pl.multiple_of(i * W, LANES), W)
            part[i, group(g), :] = (dot(gate_grad, gate[:, deep]) + dot(up_grad, up[:, deep])).astype(BF16)
            return carry

        lax.fori_loop(0, NX, column, 0)

    def reduce_1(g):
        remote(
            part.at[:, group(g), other], part_in.at[:, group(g), :], send_sem.at[12], part_recv.at[g], sibling
        ).start()

    def pair_sum(at, span):
        return part[at, span, mine].astype(F32) + part_in[at, span, :].astype(F32)

    def reduce_2(g):
        arrived(part_in.at[:, group(g), :], part_recv.at[g])
        total[0, group(g), :] = pair_sum(x_far, group(g)).astype(BF16)
        remote(
            total.at[0, pl.ds(g * NR, HALF), :], far_left.at[pl.ds(g * HALF, HALF), :], send_sem.at[13], far_recv.at[g, 0], right
        ).start()
        remote(
            total.at[0, pl.ds(g * NR + HALF, HALF), :], far_right.at[pl.ds(g * HALF, HALF), :], send_sem.at[14], far_recv.at[g, 1], left
        ).start()

    def reduce_3(g):
        half = pl.ds(g * HALF, HALF)
        lower, upper = pl.ds(g * NR, HALF), pl.ds(g * NR + HALF, HALF)
        arrived(far_left.at[half, :], far_recv.at[g, 0])
        total[1, lower, :] = (pair_sum(x_right, lower) + far_left[half, :].astype(F32)).astype(BF16)
        total[1, upper, :] = pair_sum(x_right, upper).astype(BF16)
        remote(
            total.at[1, group(g), :], near_left.at[group(g), :], send_sem.at[15], near_recv.at[g, 0], right
        ).start()
        arrived(far_right.at[half, :], far_recv.at[g, 1])
        total[2, lower, :] = pair_sum(x_left, lower).astype(BF16)
        total[2, upper, :] = (pair_sum(x_left, upper) + far_right[half, :].astype(F32)).astype(BF16)
        remote(
            total.at[2, group(g), :], near_right.at[group(g), :], send_sem.at[16], near_recv.at[g, 1], left
        ).start()

    def slots(ref, d):
        return ref.at[pl.ds(pl.multiple_of(d * CAP, CAP), CAP), :]

    own_back = pltpu.make_async_copy(slots(back, 0), slots(table, 0), one_sem.at[5])

    def reduce_4(g):
        arrived(near_left.at[group(g), :], near_recv.at[g, 0])
        arrived(near_right.at[group(g), :], near_recv.at[g, 1])
        value = near_left[group(g), :].astype(F32) + near_right[group(g), :].astype(F32)
        back[group(g), :] = (pair_sum(x, group(g)) + value).astype(BF16)

        def give(d, carry):
            remote(slots(back, d), slots(table, d), send_sem.at[17], back_recv.at[0], (back_to(d), h)).start()
            return carry

        if g == 0:
            own_back.start()
        lax.fori_loop(max(g * EG, 1), (g + 1) * EG, give, 0)

    for load in loads:
        load.wait()
    for i in range(NG + 5):
        for ahead, stage in enumerate((gather_1, gather_2, gather_3)):
            if 0 <= i - ahead < NG:
                stage(i - ahead)
        if i == NG - 1:
            scan_states()
        if 0 <= i - 2 < NG:
            expert(i - 2)
            reduce_1(i - 2)
        if i == NG + 1:
            finish_states()
        for ahead, stage in ((3, reduce_2), (4, reduce_3), (5, reduce_4)):
            if 0 <= i - ahead < NG:
                stage(i - ahead)

    own_back.wait()
    arrived(table.at[pl.ds(0, (E - 1) * CAP), :], back_recv.at[0])
    found = table[...]
    dx_ref[...] = (dot(weights[0], found) + dot(weights[1], found) + dot(weights[2], found)).astype(BF16)

    ring, half_ring = rows.at[:, 0, :, 0:DC], rows.at[0, 0, :, 0:DC]
    for i, ref in (
        (0, out_rows.at[pl.ds(1, E - 1)]),
        (1, state_out.at[pl.ds(0, (E - 1) * SR), :]),
        (2, scan_out.at[pl.ds(0, (E - 1) * SR), :]),
        (3, ring), (4, ring), (5, half_ring), (6, half_ring),
        (7, ring), (8, ring), (9, ring), (10, half_ring), (11, half_ring),
        (12, part_in), (13, far_left), (14, far_right), (15, near_left), (16, near_right),
        (17, back.at[pl.ds(0, (E - 1) * CAP), :]),
    ):
        sent(ref, send_sem.at[i])


def solution(mesh):
    E = mesh.shape["ctx"]
    NZ = min(8, E // 2)

    def shards(queries, keys, values, out_grad, log_decay, prefix_state, moe_input, moe_grad, gate, up, down, ids, probs):
        T, HL = queries.shape[0], log_decay.shape[0]
        DC, D, FL = moe_input.shape[1], gate.shape[1], gate.shape[2]
        gate, up, ids, probs = (jnp.swapaxes(array, -1, -2) for array in (gate, up, ids, probs))
        CAP = 4 * T // E
        NG = min(4, E // 2)
        ROWS, NR = E * CAP, E * CAP // NG
        vmem = pl.BlockSpec(memory_space=pltpu.VMEM)
        hbm = pl.BlockSpec(memory_space=pl.ANY)
        size = (E, E // NZ, NZ, T, CAP, DC, HL, NG)
        dma = pltpu.SemaphoreType.DMA
        return pl.pallas_call(
            functools.partial(kernel, size),
            out_shape=[jax.ShapeDtypeStruct((T, HL * LANES), BF16)] * 3 + [jax.ShapeDtypeStruct((T, DC), BF16)],
            in_specs=[vmem] * 8 + [hbm] * 3 + [vmem] * 2,
            out_specs=[vmem] * 4,
            scratch_shapes=[
                pltpu.VMEM((FL, D), BF16),
                pltpu.VMEM((FL, D), BF16),
                pltpu.VMEM((FL, D), BF16),
                pltpu.VMEM((E, 2, CAP, DC), BF16),
                pltpu.VMEM((2, NX, ROWS, 2 * DC), BF16),
                pltpu.VMEM((NR, FL), F32),
                pltpu.VMEM((NR, FL), F32),
                pltpu.VMEM((NR, FL), F32),
                pltpu.VMEM((NX, ROWS, 2 * DC), BF16),
                pltpu.VMEM((NX, ROWS, DC), BF16),
                pltpu.VMEM((3, ROWS, DC), BF16),
                pltpu.VMEM((ROWS // 2, DC), BF16),
                pltpu.VMEM((ROWS // 2, DC), BF16),
                pltpu.VMEM((ROWS, DC), BF16),
                pltpu.VMEM((ROWS, DC), BF16),
                pltpu.VMEM((ROWS, DC), BF16),
                pltpu.VMEM((ROWS, DC), BF16),
                pltpu.VMEM((3, T, ROWS), BF16),
                pltpu.VMEM((HL * LANES, 3 * LANES), BF16),
                pltpu.VMEM((HL * LANES, 3 * LANES), BF16),
                pltpu.VMEM((HL * LANES, 2 * LANES), BF16),
                pltpu.VMEM((HL * LANES, 2 * LANES), BF16),
                pltpu.VMEM((3, T, HL * LANES), F32),
                pltpu.VMEM((HL, T, LANES), F32),
                pltpu.VMEM((HL, T, LANES), F32),
                dma((3,)),
                dma((6,)),
                dma((NG,)),
                dma((NG, 4)),
                dma((NG, 5)),
                dma((18,)),
                dma((NG,)),
                dma((NG, 2)),
                dma((NG, 2)),
                dma((1,)),
            ],
            compiler_params=pltpu.CompilerParams(
                collective_id=0, has_side_effects=True, vmem_limit_bytes=52 * 1024 * 1024
            ),
        )(
            queries, keys, values, out_grad, log_decay, prefix_state.reshape(HL * LANES, LANES),
            moe_input, moe_grad, gate, up, down, ids, probs,
        )

    in_specs = (
        P("ctx", "head"),
        P("ctx", "head"),
        P("ctx", "head"),
        P("ctx", "head"),
        P("head", "ctx"),
        P("head", None, None),
        P("ctx", "head"),
        P("ctx", "head"),
        P("ctx", None, "head"),
        P("ctx", None, "head"),
        P("ctx", "head", None),
        P("ctx", None),
        P("ctx", None),
    )
    out_specs = (P("ctx", "head"), P("ctx", "head"), P("ctx", "head"), P("ctx", "head"))
    return jax.shard_map(shards, mesh=mesh, in_specs=in_specs, out_specs=out_specs, check_vma=False)
```

```python
import functools

import jax
import jax.numpy as jnp
from jax import lax
from jax.experimental import pallas as pl
from jax.experimental.pallas import tpu as pltpu
from jax.sharding import PartitionSpec as P

F32 = jnp.float32
BF16 = jnp.bfloat16
MESH = pl.DeviceIdType.MESH
NX = 4
LANES = 128


def dot(a, b):
    return jnp.dot(a, b, preferred_element_type=F32)


def dot_t(a, b):
    return lax.dot_general(a, b, (((1,), (1,)), ((), ())), preferred_element_type=F32)


def dot_l(a, b):
    return lax.dot_general(a, b, (((0,), (0,)), ((), ())), preferred_element_type=F32)


def pieces(value, count):
    parts = []
    for _ in range(count):
        part = value.astype(BF16)
        parts.append(part)
        value = value - part.astype(F32)
    return parts


def kernel(
    size,
    ids_hbm, in_hbm, grad_hbm, decay_hbm, k_hbm, v_hbm, q_hbm, g_hbm, prefix_hbm, probs_hbm, gate_hbm, up_hbm, down_hbm,
    dq_ref, dk_ref, dv_ref, dx_ref,
    ids_ref, in_ref, grad_ref, decay_ref, k_ref, v_ref, q_ref, g_ref, prefix_ref, probs_ref,
    gate, up, down, out_rows, rows, acc_gate, acc_up, acc_hidden, part, part_in, total, far_left, far_right, near_left,
    near_right, back, table, weights, state_out, state_all, scan_out, state, local, front_s, tail_s,
    load_sem, one_sem, a2a_recv, ring_recv, sib_recv, send_sem, part_recv, far_recv, near_recv, back_recv,
):
    E, NY, NZ, T, CAP, DC, HL, NG = size
    EG = E // NG
    NR = EG * CAP
    HALF = NR // 2
    W = 2 * DC
    PR = 2 * NR
    SR = HL * LANES // E
    SHIFT = NZ.bit_length() - 1

    c, h = lax.axis_index("ctx"), lax.axis_index("head")
    x, core = h // 2, h % 2
    y, z = c // NZ, c % NZ
    x_left, x_right, x_far = (x + NX - 1) % NX, (x + 1) % NX, (x + 2) % NX
    right = (c, x_right * 2 + core)
    left = (c, x_left * 2 + core)
    sibling = (c, x * 2 + 1 - core)
    mine = pl.ds(pl.multiple_of(core * DC, LANES), DC)
    other = pl.ds(pl.multiple_of((1 - core) * DC, LANES), DC)

    def forth(d):
        return ((y + d // NZ) % NY) * NZ + (z + d % NZ) % NZ

    def back_to(d):
        return ((y + NY - d // NZ) % NY) * NZ + (z + NZ - d % NZ) % NZ

    def group(g):
        return pl.ds(g * NR, NR)

    def remote(src, dst, send, recv, device):
        return pltpu.make_async_remote_copy(
            src_ref=src, dst_ref=dst, send_sem=send, recv_sem=recv, device_id=device, device_id_type=MESH
        )

    def arrived(ref, recv):
        remote(ref, ref, recv, recv, right).wait_recv()

    def sent(ref, send):
        remote(ref, ref, send, send, right).wait_send()

    barrier = pltpu.get_barrier_semaphore()

    def greet(d, carry):
        pl.semaphore_signal(barrier, inc=1, device_id=(forth(d), h), device_id_type=MESH)
        return carry

    lax.fori_loop(1, E, greet, 0)
    for device in (right, left, sibling):
        pl.semaphore_signal(barrier, inc=1, device_id=device, device_id_type=MESH)

    small = (
        (ids_hbm, ids_ref), (in_hbm, in_ref), (grad_hbm, grad_ref), (decay_hbm, decay_ref), (k_hbm, k_ref), (v_hbm, v_ref),
        (q_hbm, q_ref), (g_hbm, g_ref), (prefix_hbm, prefix_ref), (probs_hbm, probs_ref),
    )
    large = ((gate_hbm.at[0], gate), (up_hbm.at[0], up), (down_hbm.at[0], down))
    loads = [pltpu.make_async_copy(src, dst, load_sem.at[i]) for i, (src, dst) in enumerate(small + large)]
    for load in loads:
        load.start()

    for load in loads[:3]:
        load.wait()
    ahead = lax.broadcasted_iota(jnp.int32, (E, T), 0)
    expert = (((y + (ahead >> SHIFT)) & (NY - 1)) << SHIFT) + ((z + (ahead & (NZ - 1))) & (NZ - 1))
    first = (ids_ref[0:1, :] == expert).astype(F32)
    second = (ids_ref[1:2, :] == expert).astype(F32)
    named = first + second
    t_row = lax.broadcasted_iota(jnp.int32, (T, T), 0)
    t_col = lax.broadcasted_iota(jnp.int32, (T, T), 1)
    earlier = dot(named.astype(BF16), (t_row < t_col).astype(F32).astype(BF16))
    slot = jnp.where(named > 0.5, earlier, -1.0).astype(BF16)
    r_row = lax.broadcasted_iota(jnp.int32, (E * CAP, E), 0)
    e_col = lax.broadcasted_iota(jnp.int32, (E * CAP, E), 1)
    spread = (r_row // CAP == e_col).astype(F32).astype(BF16)
    want = (lax.broadcasted_iota(jnp.int32, (E * CAP, T), 0) % CAP).astype(F32)
    pick = (dot(spread, slot) == want).astype(F32).astype(BF16)
    out_rows[:, 0] = dot(pick, in_ref[...]).astype(BF16).reshape(E, CAP, DC)
    out_rows[:, 1] = dot(pick, grad_ref[...]).astype(BF16).reshape(E, CAP, DC)

    pl.semaphore_wait(barrier, E - 1 + 3)

    def dispatch(d, carry):
        remote(
            out_rows.at[d], rows.at[:, x, pl.ds(d * CAP, CAP), mine], send_sem.at[0], a2a_recv.at[d // EG], (forth(d), h)
        ).start()
        return carry

    own = pltpu.make_async_copy(out_rows.at[0], rows.at[:, x, pl.ds(0, CAP), mine], one_sem.at[0])
    own.start()
    lax.fori_loop(1, E, dispatch, 0)

    for load in loads[3:8]:
        load.wait()
    cum = jnp.zeros((HL, T), F32)
    upto = (t_row <= t_col).astype(F32).astype(BF16)
    for piece in pieces(decay_ref[...], 3):
        cum = cum + dot(piece, upto)
    slab = lax.broadcasted_iota(jnp.int32, (LANES, LANES), 0) % SR
    for i in range(HL):
        cols = slice(i * LANES, (i + 1) * LANES)
        along = jnp.broadcast_to(cum[i : i + 1, :], (T, T))
        down_t = along.T
        total_b = jnp.broadcast_to(down_t[T - 1 : T, :], (T, T))
        front_s[i] = jnp.exp(down_t)
        tail_s[i] = jnp.exp(total_b - down_t)
        q, k, v, g = q_ref[:, cols], k_ref[:, cols], v_ref[:, cols], g_ref[:, cols]
        state_out[cols, 0:LANES] = dot_l((k.astype(F32) * tail_s[i]).astype(BF16), v).astype(BF16)
        state_out[cols, LANES : 2 * LANES] = dot_l((q.astype(F32) * front_s[i]).astype(BF16), g).astype(BF16)
        d0, d1, d2 = [piece.astype(F32) for piece in pieces(jnp.exp(total_b), 3)]
        state_out[cols, 2 * LANES :] = jnp.where(slab == 0, d0, jnp.where(slab == 1, d1, d2)).astype(BF16)

    def slices(ref, p):
        return ref.at[pl.ds(pl.multiple_of(p * SR, SR), SR), :]

    def states(d, carry):
        remote(slices(state_out, forth(d)), slices(state_all, c), send_sem.at[1], one_sem.at[1], (forth(d), h)).start()
        return carry

    own_state = pltpu.make_async_copy(slices(state_out, c), slices(state_all, c), one_sem.at[2])
    own_state.start()
    lax.fori_loop(1, E, states, 0)

    def within_block(i):
        cols = slice(i * LANES, (i + 1) * LANES)
        along = jnp.broadcast_to(cum[i : i + 1, :], (T, T))
        down_t = along.T
        q, k, v, g = q_ref[:, cols], k_ref[:, cols], v_ref[:, cols], g_ref[:, cols]
        low, high = t_row >= t_col, t_row <= t_col
        within = jnp.where(low, jnp.exp(jnp.where(low, down_t - along, 0.0)), 0.0)
        within_t = jnp.where(high, jnp.exp(jnp.where(high, along - down_t, 0.0)), 0.0)
        local[0, :, cols] = dot((dot_t(g, v) * within).astype(BF16), k)
        local[1, :, cols] = dot((dot_t(v, g) * within_t).astype(BF16), q)
        local[2, :, cols] = dot((dot_t(k, q) * within_t).astype(BF16), g)

    def weigh(_):
        loads[9].wait()
        chance = first * probs_ref[0:1, :] + second * probs_ref[1:2, :]
        r_col = lax.broadcasted_iota(jnp.int32, (E, E * CAP), 1)
        spread_t = (r_col // CAP == lax.broadcasted_iota(jnp.int32, (E, E * CAP), 0)).astype(F32).astype(BF16)
        pick_t = dot_l(slot, spread_t) == (lax.broadcasted_iota(jnp.int32, (T, E * CAP), 1) % CAP).astype(F32)
        for i, piece in enumerate(pieces(chance, 3)):
            weights[i] = jnp.where(pick_t, dot_l(piece, spread_t), 0.0).astype(BF16)

    def scan_states(_):
        loads[8].wait()
        own_state.wait()
        arrived(state_all.at[pl.ds(0, (E - 1) * SR), :], one_sem.at[1])

        def step(i, carried):
            new = []
            for column, (at, value) in enumerate(zip((i, E - 1 - i), carried)):
                tile = slices(state_all, at)[...].astype(F32)
                factor = tile[0:1, 2 * LANES :] + tile[1:2, 2 * LANES :] + tile[2:3, 2 * LANES :]
                columns = slice(column * LANES, (column + 1) * LANES)
                slices(scan_out, at)[:, columns] = value.astype(BF16)
                new.append(factor * value + tile[:, columns])
            return tuple(new)

        lax.fori_loop(0, E, step, (slices(prefix_ref, c)[...], jnp.zeros((SR, LANES), F32)), unroll=4)

        def give(d, carry):
            remote(slices(scan_out, forth(d)), slices(state, c), send_sem.at[2], one_sem.at[3], (forth(d), h)).start()
            return carry

        own_scan.start()
        lax.fori_loop(1, E, give, 0)

    own_scan = pltpu.make_async_copy(slices(scan_out, c), slices(state, c), one_sem.at[4])

    def finish_states(i):
        if i == 0:
            own_scan.wait()
            arrived(state.at[pl.ds(0, (E - 1) * SR), :], one_sem.at[3])
        cols = slice(i * LANES, (i + 1) * LANES)
        k, v, g = k_ref[:, cols], v_ref[:, cols], g_ref[:, cols]
        s_in, s_grad = state[cols, 0:LANES], state[cols, LANES : 2 * LANES]
        dq_ref[:, cols] = (local[0, :, cols] + front_s[i] * dot_t(g, s_in)).astype(BF16)
        dk_ref[:, cols] = (local[1, :, cols] + tail_s[i] * dot_t(v, s_grad)).astype(BF16)
        dv_ref[:, cols] = (local[2, :, cols] + tail_s[i] * dot(k, s_grad)).astype(BF16)

    def to_sibling(ref, which, send):
        remote(ref, ref, send_sem.at[send], sib_recv.at[which], sibling).start()

    def gather_1(g):
        if g == 0:
            own.wait()
        lead = CAP if g == 0 else 0
        arrived(rows.at[:, x, pl.ds(g * NR + lead, NR - lead), mine], a2a_recv.at[g])
        ref = rows.at[:, x, group(g), mine]
        remote(ref, ref, send_sem.at[3], ring_recv.at[g, 0], right).start()
        remote(ref, ref, send_sem.at[4], ring_recv.at[g, 1], left).start()
        to_sibling(ref, (g, 0), 7)

    def gather_2(g):
        from_left, from_right = rows.at[:, x_left, group(g), mine], rows.at[:, x_right, group(g), mine]
        arrived(from_left, ring_recv.at[g, 0])
        ref = rows.at[0, x_left, group(g), mine]
        remote(ref, ref, send_sem.at[5], ring_recv.at[g, 2], right).start()
        to_sibling(from_left, (g, 1), 8)
        arrived(from_right, ring_recv.at[g, 1])
        ref = rows.at[1, x_right, group(g), mine]
        remote(ref, ref, send_sem.at[6], ring_recv.at[g, 3], left).start()
        to_sibling(from_right, (g, 2), 9)

    def gather_3(g):
        for i in range(2):
            ref = rows.at[i, x_far, group(g), mine]
            arrived(ref, ring_recv.at[g, 2 + i])
            to_sibling(ref, (g, 3 + i), 10 + i)

    def expert_in(p, i):
        at = (x, x_left, x_right, x_far)[i]
        for g in (2 * p, 2 * p + 1):
            if i < 3:
                arrived(rows.at[:, at, group(g), other], sib_recv.at[g, i])
            else:
                arrived(rows.at[0, at, group(g), other], sib_recv.at[g, 3])
                arrived(rows.at[1, at, group(g), other], sib_recv.at[g, 4])
        if p == 0 and i == 0:
            for load in loads[10:]:
                load.wait()
        deep = pl.ds(pl.multiple_of(at * W, LANES), W)
        r_in, r_grad = rows[0, at, pl.ds(p * PR, PR), :], rows[1, at, pl.ds(p * PR, PR), :]
        for acc, r, weight in ((acc_gate, r_in, gate), (acc_up, r_in, up), (acc_hidden, r_grad, down)):
            value = dot_t(r, weight[:, deep])
            acc[p] = value if i == 0 else acc[p] + value

    def expert_out(p):
        gate_pre, up_pre, hidden = acc_gate[p], acc_up[p], acc_hidden[p]
        sig = 1.0 / (1.0 + jnp.exp(-gate_pre))
        gate_grad = (hidden * up_pre * sig * (1.0 + gate_pre * (1.0 - sig))).astype(BF16)
        up_grad = (hidden * gate_pre * sig).astype(BF16)
        span = pl.ds(p * PR, PR)
        for i, at in enumerate((x_far, x_right, x_left, x)):
            deep = pl.ds(pl.multiple_of(at * W, LANES), W)
            part[at, span, :] = (dot(gate_grad, gate[:, deep]) + dot(up_grad, up[:, deep])).astype(BF16)
            remote(
                part.at[at, span, other], part_in.at[at, span, :], send_sem.at[12], part_recv.at[p, i], sibling
            ).start()

    def from_sibling(g, i, at):
        if g % 2 == 0:
            arrived(part_in.at[at, pl.ds(g * NR, PR), :], part_recv.at[g // 2, i])

    def pair_sum(at, span):
        return part[at, span, mine].astype(F32) + part_in[at, span, :].astype(F32)

    def reduce_2(g):
        from_sibling(g, 0, x_far)
        total[0, group(g), :] = pair_sum(x_far, group(g)).astype(BF16)
        remote(
            total.at[0, pl.ds(g * NR, HALF), :], far_left.at[pl.ds(g * HALF, HALF), :], send_sem.at[13], far_recv.at[g, 0], right
        ).start()
        remote(
            total.at[0, pl.ds(g * NR + HALF, HALF), :], far_right.at[pl.ds(g * HALF, HALF), :], send_sem.at[14], far_recv.at[g, 1], left
        ).start()

    def reduce_3(g):
        half = pl.ds(g * HALF, HALF)
        lower, upper = pl.ds(g * NR, HALF), pl.ds(g * NR + HALF, HALF)
        from_sibling(g, 1, x_right)
        arrived(far_left.at[half, :], far_recv.at[g, 0])
        total[1, lower, :] = (pair_sum(x_right, lower) + far_left[half, :].astype(F32)).astype(BF16)
        total[1, upper, :] = pair_sum(x_right, upper).astype(BF16)
        remote(
            total.at[1, group(g), :], near_left.at[group(g), :], send_sem.at[15], near_recv.at[g, 0], right
        ).start()
        from_sibling(g, 2, x_left)
        arrived(far_right.at[half, :], far_recv.at[g, 1])
        total[2, lower, :] = pair_sum(x_left, lower).astype(BF16)
        total[2, upper, :] = (pair_sum(x_left, upper) + far_right[half, :].astype(F32)).astype(BF16)
        remote(
            total.at[2, group(g), :], near_right.at[group(g), :], send_sem.at[16], near_recv.at[g, 1], left
        ).start()

    def slots(ref, d):
        return ref.at[pl.ds(pl.multiple_of(d * CAP, CAP), CAP), :]

    own_back = pltpu.make_async_copy(slots(back, 0), slots(table, 0), one_sem.at[5])

    def reduce_4(g):
        from_sibling(g, 3, x)
        arrived(near_left.at[group(g), :], near_recv.at[g, 0])
        arrived(near_right.at[group(g), :], near_recv.at[g, 1])
        value = near_left[group(g), :].astype(F32) + near_right[group(g), :].astype(F32)
        back[group(g), :] = (pair_sum(x, group(g)) + value).astype(BF16)

        def give(d, carry):
            remote(slots(back, d), slots(table, d), send_sem.at[17], back_recv.at[0], (back_to(d), h)).start()
            return carry

        if g == 0:
            own_back.start()
        lax.fori_loop(max(g * EG, 1), (g + 1) * EG, give, 0)

    last = 20.5 + 9.6 * (NG // 2 - 1)
    plan = [(last - 6.6, scan_states, 0), (16.5, weigh, 0)]
    for g in range(NG):
        plan += [(4 + 4 * g, gather_1, g), (9 + 5.2 * g, gather_2, g), (14.6 + 4.8 * g, gather_3, g)]
    for i, at in enumerate((5, 6, 13, 13.1)[:HL]):
        plan.append((at, within_block, i))
    for p in range(NG // 2):
        for i, at in enumerate((9.5 + 8 * p, 15.4 + 10.4 * p, 15.5 + 10.4 * p, 20.4 + 9.6 * p)):
            plan.append((at, functools.partial(expert_in, p), i))
        out = 20.5 + 9.6 * p
        plan.append((out, expert_out, p))
        for g in (0, 1):
            for stage, at in ((reduce_2, 2 + g * 0.1), (reduce_3, 4.5 + g * 0.1), (reduce_4, 8 + g)):
                plan.append((out + at, stage, 2 * p + g))
    for i in range(HL):
        plan.append((last + (2.5, 2.6, 5, 5.1)[i], finish_states, i))
    for _, stage, which in sorted(plan, key=lambda entry: entry[0]):
        stage(which)

    own_back.wait()
    arrived(table.at[pl.ds(0, (E - 1) * CAP), :], back_recv.at[0])
    found = table[...]
    dx_ref[...] = (dot(weights[0], found) + dot(weights[1], found) + dot(weights[2], found)).astype(BF16)

    ring, half_ring = rows.at[:, 0, :, 0:DC], rows.at[0, 0, :, 0:DC]
    for i, ref in (
        (0, out_rows.at[pl.ds(1, E - 1)]),
        (1, state_out.at[pl.ds(0, (E - 1) * SR), :]),
        (2, scan_out.at[pl.ds(0, (E - 1) * SR), :]),
        (3, ring), (4, ring), (5, half_ring), (6, half_ring),
        (7, ring), (8, ring), (9, ring), (10, half_ring), (11, half_ring),
        (12, part_in), (13, far_left), (14, far_right), (15, near_left), (16, near_right),
        (17, back.at[pl.ds(0, (E - 1) * CAP), :]),
    ):
        sent(ref, send_sem.at[i])


def copy_out(*refs):
    copies = [pltpu.make_async_copy(refs[i], refs[4 + i], refs[8].at[i]) for i in range(4)]
    for copy in copies:
        copy.start()
    for copy in copies:
        copy.wait()


def solution(mesh):
    E = mesh.shape["ctx"]
    NZ = min(8, E // 2)

    def shards(queries, keys, values, out_grad, log_decay, prefix_state, moe_input, moe_grad, gate, up, down, ids, probs):
        T, HL = queries.shape[0], log_decay.shape[0]
        DC, D, FL = moe_input.shape[1], gate.shape[1], gate.shape[2]
        gate, up, ids, probs = (jnp.swapaxes(array, -1, -2) for array in (gate, up, ids, probs))
        CAP = 4 * T // E
        NG = min(4, E // 2)
        ROWS, NR = E * CAP, E * CAP // NG
        vmem = pl.BlockSpec(memory_space=pltpu.VMEM)
        hbm = pl.BlockSpec(memory_space=pltpu.HBM)
        size = (E, E // NZ, NZ, T, CAP, DC, HL, NG)
        dma = pltpu.SemaphoreType.DMA
        results = [jax.ShapeDtypeStruct((T, HL * LANES), BF16)] * 3 + [jax.ShapeDtypeStruct((T, DC), BF16)]
        small = (
            ids, moe_input, moe_grad, log_decay, keys, values, queries, out_grad,
            prefix_state.reshape(HL * LANES, LANES), probs,
        )
        made = pl.pallas_call(
            functools.partial(kernel, size),
            out_shape=results,
            in_specs=[hbm] * 13,
            out_specs=[vmem] * 4,
            scratch_shapes=[pltpu.VMEM(array.shape, array.dtype) for array in small]
            + [
                pltpu.VMEM((FL, D), BF16),
                pltpu.VMEM((FL, D), BF16),
                pltpu.VMEM((FL, D), BF16),
                pltpu.VMEM((E, 2, CAP, DC), BF16),
                pltpu.VMEM((2, NX, ROWS, 2 * DC), BF16),
                pltpu.VMEM((NG // 2, 2 * NR, FL), F32),
                pltpu.VMEM((NG // 2, 2 * NR, FL), F32),
                pltpu.VMEM((NG // 2, 2 * NR, FL), F32),
                pltpu.VMEM((NX, ROWS, 2 * DC), BF16),
                pltpu.VMEM((NX, ROWS, DC), BF16),
                pltpu.VMEM((3, ROWS, DC), BF16),
                pltpu.VMEM((ROWS // 2, DC), BF16),
                pltpu.VMEM((ROWS // 2, DC), BF16),
                pltpu.VMEM((ROWS, DC), BF16),
                pltpu.VMEM((ROWS, DC), BF16),
                pltpu.VMEM((ROWS, DC), BF16),
                pltpu.VMEM((ROWS, DC), BF16),
                pltpu.VMEM((3, T, ROWS), BF16),
                pltpu.VMEM((HL * LANES, 3 * LANES), BF16),
                pltpu.VMEM((HL * LANES, 3 * LANES), BF16),
                pltpu.VMEM((HL * LANES, 2 * LANES), BF16),
                pltpu.VMEM((HL * LANES, 2 * LANES), BF16),
                pltpu.VMEM((3, T, HL * LANES), F32),
                pltpu.VMEM((HL, T, LANES), F32),
                pltpu.VMEM((HL, T, LANES), F32),
                dma((13,)),
                dma((6,)),
                dma((NG,)),
                dma((NG, 4)),
                dma((NG, 5)),
                dma((18,)),
                dma((NG // 2, 4)),
                dma((NG, 2)),
                dma((NG, 2)),
                dma((1,)),
            ],
            compiler_params=pltpu.CompilerParams(
                collective_id=0, has_side_effects=True, vmem_limit_bytes=52 * 1024 * 1024
            ),
        )(*(pltpu.with_memory_space_constraint(array, pltpu.HBM) for array in (*small, gate, up, down)))
        return pl.pallas_call(
            copy_out,
            out_shape=results,
            in_specs=[vmem] * 4,
            out_specs=[hbm] * 4,
            scratch_shapes=[dma((4,))],
        )(*(pltpu.with_memory_space_constraint(array, pltpu.VMEM) for array in made))

    in_specs = (
        P("ctx", "head"),
        P("ctx", "head"),
        P("ctx", "head"),
        P("ctx", "head"),
        P("head", "ctx"),
        P("head", None, None),
        P("ctx", "head"),
        P("ctx", "head"),
        P("ctx", None, "head"),
        P("ctx", None, "head"),
        P("ctx", "head", None),
        P("ctx", None),
        P("ctx", None),
    )
    out_specs = (P("ctx", "head"), P("ctx", "head"), P("ctx", "head"), P("ctx", "head"))
    return jax.shard_map(shards, mesh=mesh, in_specs=in_specs, out_specs=out_specs, check_vma=False)
```

```python
import functools

import jax
import jax.numpy as jnp
from jax import lax
from jax.experimental import pallas as pl
from jax.experimental.pallas import tpu as pltpu
from jax.sharding import PartitionSpec as P

F32 = jnp.float32
BF16 = jnp.bfloat16
MESH = pl.DeviceIdType.MESH
NX = 4
LANES = 128


def dot(a, b):
    return jnp.dot(a, b, preferred_element_type=F32)


def dot_t(a, b):
    return lax.dot_general(a, b, (((1,), (1,)), ((), ())), preferred_element_type=F32)


def dot_l(a, b):
    return lax.dot_general(a, b, (((0,), (0,)), ((), ())), preferred_element_type=F32)


def pieces(value, count):
    parts = []
    for _ in range(count):
        part = value.astype(BF16)
        parts.append(part)
        value = value - part.astype(F32)
    return parts


RANK = dict(s1=0, s2=0, s3=0, r2=1, near=1, r3=1, r4=1, mix=4, mid=2, out=2, scan=2.5, finish=3.5, within=4, weigh=4)
RANK["in"] = 2


def order(groups, rank):
    pairs, q = groups // 2, 4.0 / groups
    stages = {}

    def add(name, cost, needs, sends=()):
        stages[name] = (cost, needs, sends)

    came = {("disp", g): 1.0 + 5.6 * q * (g + 1) for g in range(groups)}
    came["states"] = 1.0 + 5.6 * q * groups + 4
    free = {"x": 0.0, "sib": 0.0, "z": came["states"]}
    for g in range(groups):
        p = g // 2
        add(("s1", g), 0.2, [("disp", g)], [(("l1", g), "x", 4.4 * q), (("b", 0, g), "sib", 0.8 * q)])
        add(("s2", g), 0.3, [("l1", g)], [(("l2", g), "x", 2.2 * q), (("b", 1, g), "sib", 0.8 * q), (("b", 2, g), "sib", 0.8 * q)])
        add(("s3", g), 0.3, [("l2", g)], [(("b", 3, g), "sib", 0.8 * q)])
        add(("r2", g), 0.4, [("c", p, 0)], [(("f", g), "x", 1.1 * q)])
        add(("near", g), 0.3, [("c", p, 1), ("c", p, 2)], [(("m", g), "x", 1.1 * q)])
        add(("r3", g), 0.4, [("f", g), ("c", p, 1), ("c", p, 2)], [(("n", g), "x", 1.1 * q)])
        add(("r4", g), 0.7, [("m", g), ("n", g), ("c", p, 3)], [(("t", g), "z", 2.2 * q)])
    for p in range(pairs):
        for i in range(4):
            add(("in", p, i), 1.05 * q, [("b", i, 2 * p), ("b", i, 2 * p + 1)] + [("in", p, j) for j in range(i)])
            add(("out", p, i), 0.7 * q, [("mid", p)] + [("out", p, j) for j in range(i)], [(("c", p, i), "sib", 0.5)])
        add(("mix", p), 0.5, [("t", 2 * p), ("t", 2 * p + 1), ("weigh",)])
        add(("mid", p), 0.4 * q, [("in", p, i) for i in range(4)])
    for i in range(4):
        add(("within", i), 0.9, [])
        add(("finish", i), 0.5, ["scanned", ("within", i)])
    add(("weigh",), 1.0, [])
    add(("scan",), 2.0, ["states"], [("scanned", "z", 5.5)])
    done, now = [], 3.0
    while len(done) < len(stages):
        ready = []
        for name, (cost, needs, sends) in stages.items():
            if name not in done and all(n in came for n in needs):
                ready.append((max([0.0] + [came[n] for n in needs]), name))
        start = min(at for at, _ in ready)
        now = max(now, start)
        _, name = min((rank[name[0]] + 0.01 * sum(name[1:2]), name) for at, name in ready if at <= now)
        cost, needs, sends = stages[name]
        now += cost
        done.append(name)
        came[name] = now
        for event, link, took in sends:
            free[link] = max(free[link], now) + took
            came[event] = free[link] + 1.6
    return done


def kernel(
    size,
    ids_hbm, in_hbm, grad_hbm, decay_hbm, k_hbm, v_hbm, q_hbm, g_hbm, prefix_hbm, probs_hbm, gate_hbm, up_hbm, down_hbm,
    dq_ref, dk_ref, dv_ref, dx_ref,
    ids_ref, in_ref, grad_ref, decay_ref, k_ref, v_ref, q_ref, g_ref, prefix_ref, probs_ref,
    gate, up, down, out_rows, rows, acc_gate, acc_up, acc_hidden, gate_s, up_s, mixed, part, part_in, total, far_left, far_right, near_left,
    near_right, back, table, weights, state_out, state_all, scan_out, state, local, front_s, tail_s,
    load_sem, one_sem, a2a_recv, ring_recv, sib_recv, send_sem, part_recv, far_recv, near_recv, back_recv,
):
    E, NY, NZ, T, CAP, DC, HL, NG = size
    EG = E // NG
    NR = EG * CAP
    HALF = NR // 2
    W = 2 * DC
    PR = 2 * NR
    SR = HL * LANES // E
    SHIFT = NZ.bit_length() - 1

    c, h = lax.axis_index("ctx"), lax.axis_index("head")
    x, core = h // 2, h % 2
    y, z = c // NZ, c % NZ
    x_left, x_right, x_far = (x + NX - 1) % NX, (x + 1) % NX, (x + 2) % NX
    right = (c, x_right * 2 + core)
    left = (c, x_left * 2 + core)
    sibling = (c, x * 2 + 1 - core)
    mine = pl.ds(pl.multiple_of(core * DC, LANES), DC)
    other = pl.ds(pl.multiple_of((1 - core) * DC, LANES), DC)

    def forth(d):
        return ((y + d // NZ) % NY) * NZ + (z + d % NZ) % NZ

    def back_to(d):
        return ((y + NY - d // NZ) % NY) * NZ + (z + NZ - d % NZ) % NZ

    def group(g):
        return pl.ds(g * NR, NR)

    def remote(src, dst, send, recv, device):
        return pltpu.make_async_remote_copy(
            src_ref=src, dst_ref=dst, send_sem=send, recv_sem=recv, device_id=device, device_id_type=MESH
        )

    def arrived(ref, recv):
        remote(ref, ref, recv, recv, right).wait_recv()

    def sent(ref, send):
        remote(ref, ref, send, send, right).wait_send()

    barrier = pltpu.get_barrier_semaphore()

    def greet(d, carry):
        pl.semaphore_signal(barrier, inc=1, device_id=(forth(d), h), device_id_type=MESH)
        return carry

    lax.fori_loop(1, E, greet, 0)
    for device in (right, left, sibling):
        pl.semaphore_signal(barrier, inc=1, device_id=device, device_id_type=MESH)

    small = (
        (ids_hbm, ids_ref), (in_hbm, in_ref), (grad_hbm, grad_ref), (decay_hbm, decay_ref), (k_hbm, k_ref), (v_hbm, v_ref),
        (q_hbm, q_ref), (g_hbm, g_ref), (prefix_hbm, prefix_ref), (probs_hbm, probs_ref),
    )
    large = ((gate_hbm.at[0], gate), (up_hbm.at[0], up), (down_hbm.at[0], down))
    loads = [pltpu.make_async_copy(src, dst, load_sem.at[i]) for i, (src, dst) in enumerate(small + large)]
    for load in loads:
        load.start()

    for load in loads[:3]:
        load.wait()
    ahead = lax.broadcasted_iota(jnp.int32, (E, T), 0)
    expert = (((y + (ahead >> SHIFT)) & (NY - 1)) << SHIFT) + ((z + (ahead & (NZ - 1))) & (NZ - 1))
    first = (ids_ref[0:1, :] == expert).astype(F32)
    second = (ids_ref[1:2, :] == expert).astype(F32)
    named = first + second
    t_row = lax.broadcasted_iota(jnp.int32, (T, T), 0)
    t_col = lax.broadcasted_iota(jnp.int32, (T, T), 1)
    earlier = dot(named.astype(BF16), (t_row < t_col).astype(F32).astype(BF16))
    slot = jnp.where(named > 0.5, earlier, -1.0).astype(BF16)
    r_row = lax.broadcasted_iota(jnp.int32, (E * CAP, E), 0)
    e_col = lax.broadcasted_iota(jnp.int32, (E * CAP, E), 1)
    spread = (r_row // CAP == e_col).astype(F32).astype(BF16)
    want = (lax.broadcasted_iota(jnp.int32, (E * CAP, T), 0) % CAP).astype(F32)
    pick = (dot(spread, slot) == want).astype(F32).astype(BF16)
    out_rows[:, 0] = dot(pick, in_ref[...]).astype(BF16).reshape(E, CAP, DC)
    out_rows[:, 1] = dot(pick, grad_ref[...]).astype(BF16).reshape(E, CAP, DC)

    pl.semaphore_wait(barrier, E - 1 + 3)

    def dispatch(d, carry):
        remote(
            out_rows.at[d], rows.at[:, x, pl.ds(d * CAP, CAP), mine], send_sem.at[0], a2a_recv.at[d // EG], (forth(d), h)
        ).start()
        return carry

    own = pltpu.make_async_copy(out_rows.at[0], rows.at[:, x, pl.ds(0, CAP), mine], one_sem.at[0])
    own.start()
    lax.fori_loop(1, E, dispatch, 0)

    for load in loads[3:8]:
        load.wait()
    cum = jnp.zeros((HL, T), F32)
    upto = (t_row <= t_col).astype(F32).astype(BF16)
    for piece in pieces(decay_ref[...], 3):
        cum = cum + dot(piece, upto)
    slab = lax.broadcasted_iota(jnp.int32, (LANES, LANES), 0) % SR
    for i in range(HL):
        cols = slice(i * LANES, (i + 1) * LANES)
        along = jnp.broadcast_to(cum[i : i + 1, :], (T, T))
        down_t = along.T
        total_b = jnp.broadcast_to(down_t[T - 1 : T, :], (T, T))
        front_s[i] = jnp.exp(down_t)
        tail_s[i] = jnp.exp(total_b - down_t)
        q, k, v, g = q_ref[:, cols], k_ref[:, cols], v_ref[:, cols], g_ref[:, cols]
        state_out[cols, 0:LANES] = dot_l((k.astype(F32) * tail_s[i]).astype(BF16), v).astype(BF16)
        state_out[cols, LANES : 2 * LANES] = dot_l((q.astype(F32) * front_s[i]).astype(BF16), g).astype(BF16)
        d0, d1, d2 = [piece.astype(F32) for piece in pieces(jnp.exp(total_b), 3)]
        state_out[cols, 2 * LANES :] = jnp.where(slab == 0, d0, jnp.where(slab == 1, d1, d2)).astype(BF16)

    def slices(ref, p):
        return ref.at[pl.ds(pl.multiple_of(p * SR, SR), SR), :]

    def states(d, carry):
        remote(slices(state_out, forth(d)), slices(state_all, c), send_sem.at[1], one_sem.at[1], (forth(d), h)).start()
        return carry

    own_state = pltpu.make_async_copy(slices(state_out, c), slices(state_all, c), one_sem.at[2])
    own_state.start()
    lax.fori_loop(1, E, states, 0)

    seen = set()

    def within_block(i):
        cols = slice(i * LANES, (i + 1) * LANES)
        along = jnp.broadcast_to(cum[i : i + 1, :], (T, T))
        down_t = along.T
        q, k, v, g = q_ref[:, cols], k_ref[:, cols], v_ref[:, cols], g_ref[:, cols]
        low, high = t_row >= t_col, t_row <= t_col
        within = jnp.where(low, jnp.exp(jnp.where(low, down_t - along, 0.0)), 0.0)
        within_t = jnp.where(high, jnp.exp(jnp.where(high, along - down_t, 0.0)), 0.0)
        local[0, :, cols] = dot((dot_t(g, v) * within).astype(BF16), k)
        local[1, :, cols] = dot((dot_t(v, g) * within_t).astype(BF16), q)
        local[2, :, cols] = dot((dot_t(k, q) * within_t).astype(BF16), g)

    def weigh():
        loads[9].wait()
        chance = first * probs_ref[0:1, :] + second * probs_ref[1:2, :]
        r_col = lax.broadcasted_iota(jnp.int32, (E, E * CAP), 1)
        spread_t = (r_col // CAP == lax.broadcasted_iota(jnp.int32, (E, E * CAP), 0)).astype(F32).astype(BF16)
        pick_t = dot_l(slot, spread_t) == (lax.broadcasted_iota(jnp.int32, (T, E * CAP), 1) % CAP).astype(F32)
        for i, piece in enumerate(pieces(chance, 3)):
            weights[i] = jnp.where(pick_t, dot_l(piece, spread_t), 0.0).astype(BF16)

    def scan_states():
        loads[8].wait()
        own_state.wait()
        arrived(state_all.at[pl.ds(0, (E - 1) * SR), :], one_sem.at[1])

        def step(i, carried):
            new = []
            for column, (at, value) in enumerate(zip((i, E - 1 - i), carried)):
                tile = slices(state_all, at)[...].astype(F32)
                factor = tile[0:1, 2 * LANES :] + tile[1:2, 2 * LANES :] + tile[2:3, 2 * LANES :]
                columns = slice(column * LANES, (column + 1) * LANES)
                slices(scan_out, at)[:, columns] = value.astype(BF16)
                new.append(factor * value + tile[:, columns])
            return tuple(new)

        lax.fori_loop(0, E, step, (slices(prefix_ref, c)[...], jnp.zeros((SR, LANES), F32)), unroll=4)

        def give(d, carry):
            remote(slices(scan_out, forth(d)), slices(state, c), send_sem.at[2], one_sem.at[3], (forth(d), h)).start()
            return carry

        own_scan.start()
        lax.fori_loop(1, E, give, 0)

    own_scan = pltpu.make_async_copy(slices(scan_out, c), slices(state, c), one_sem.at[4])

    def finish_states(i):
        if "state" not in seen:
            seen.add("state")
            own_scan.wait()
            arrived(state.at[pl.ds(0, (E - 1) * SR), :], one_sem.at[3])
        cols = slice(i * LANES, (i + 1) * LANES)
        k, v, g = k_ref[:, cols], v_ref[:, cols], g_ref[:, cols]
        s_in, s_grad = state[cols, 0:LANES], state[cols, LANES : 2 * LANES]
        dq_ref[:, cols] = (local[0, :, cols] + front_s[i] * dot_t(g, s_in)).astype(BF16)
        dk_ref[:, cols] = (local[1, :, cols] + tail_s[i] * dot_t(v, s_grad)).astype(BF16)
        dv_ref[:, cols] = (local[2, :, cols] + tail_s[i] * dot(k, s_grad)).astype(BF16)

    def to_sibling(ref, which, send):
        remote(ref, ref, send_sem.at[send], sib_recv.at[which], sibling).start()

    def gather_1(g):
        if g == 0:
            own.wait()
        lead = CAP if g == 0 else 0
        arrived(rows.at[:, x, pl.ds(g * NR + lead, NR - lead), mine], a2a_recv.at[g])
        ref = rows.at[:, x, group(g), mine]
        remote(ref, ref, send_sem.at[3], ring_recv.at[g, 0], right).start()
        remote(ref, ref, send_sem.at[4], ring_recv.at[g, 1], left).start()
        to_sibling(ref, (g, 0), 7)

    def gather_2(g):
        from_left, from_right = rows.at[:, x_left, group(g), mine], rows.at[:, x_right, group(g), mine]
        arrived(from_left, ring_recv.at[g, 0])
        ref = rows.at[0, x_left, group(g), mine]
        remote(ref, ref, send_sem.at[5], ring_recv.at[g, 2], right).start()
        to_sibling(from_left, (g, 1), 8)
        arrived(from_right, ring_recv.at[g, 1])
        ref = rows.at[1, x_right, group(g), mine]
        remote(ref, ref, send_sem.at[6], ring_recv.at[g, 3], left).start()
        to_sibling(from_right, (g, 2), 9)

    def gather_3(g):
        for i in range(2):
            ref = rows.at[i, x_far, group(g), mine]
            arrived(ref, ring_recv.at[g, 2 + i])
            to_sibling(ref, (g, 3 + i), 10 + i)

    def expert_in(p, i):
        at = (x, x_left, x_right, x_far)[i]
        for g in (2 * p, 2 * p + 1):
            if i < 3:
                arrived(rows.at[:, at, group(g), other], sib_recv.at[g, i])
            else:
                arrived(rows.at[0, at, group(g), other], sib_recv.at[g, 3])
                arrived(rows.at[1, at, group(g), other], sib_recv.at[g, 4])
        if "weights" not in seen:
            seen.add("weights")
            for load in loads[10:]:
                load.wait()
        deep = pl.ds(pl.multiple_of(at * W, LANES), W)
        r_in, r_grad = rows[0, at, pl.ds(p * PR, PR), :], rows[1, at, pl.ds(p * PR, PR), :]
        for acc, r, weight in ((acc_gate, r_in, gate), (acc_up, r_in, up), (acc_hidden, r_grad, down)):
            value = dot_t(r, weight[:, deep])
            acc[p] = value if i == 0 else acc[p] + value

    def expert_mid(p):
        gate_pre, up_pre, hidden = acc_gate[p], acc_up[p], acc_hidden[p]
        sig = 1.0 / (1.0 + jnp.exp(-gate_pre))
        gate_s[p] = (hidden * up_pre * sig * (1.0 + gate_pre * (1.0 - sig))).astype(BF16)
        up_s[p] = (hidden * gate_pre * sig).astype(BF16)

    def expert_out(p, i):
        at = (x_far, x_right, x_left, x)[i]
        span = pl.ds(p * PR, PR)
        deep = pl.ds(pl.multiple_of(at * W, LANES), W)
        part[at, span, :] = (dot(gate_s[p], gate[:, deep]) + dot(up_s[p], up[:, deep])).astype(BF16)
        remote(
            part.at[at, span, other], part_in.at[at, span, :], send_sem.at[12], part_recv.at[p, i], sibling
        ).start()

    def from_sibling(g, i, at):
        if (g // 2, i) not in seen:
            seen.add((g // 2, i))
            arrived(part_in.at[at, pl.ds(g * NR, PR), :], part_recv.at[g // 2, i])

    def pair_sum(at, span):
        return part[at, span, mine].astype(F32) + part_in[at, span, :].astype(F32)

    def reduce_2(g):
        from_sibling(g, 0, x_far)
        total[0, group(g), :] = pair_sum(x_far, group(g)).astype(BF16)
        remote(
            total.at[0, pl.ds(g * NR, HALF), :], far_left.at[pl.ds(g * HALF, HALF), :], send_sem.at[13], far_recv.at[g, 0], right
        ).start()
        remote(
            total.at[0, pl.ds(g * NR + HALF, HALF), :], far_right.at[pl.ds(g * HALF, HALF), :], send_sem.at[14], far_recv.at[g, 1], left
        ).start()

    def halves(g):
        return pl.ds(g * NR, HALF), pl.ds(g * NR + HALF, HALF)

    def to_right(span, recv):
        remote(total.at[1, span, :], near_left.at[span, :], send_sem.at[15], recv, right).start()

    def to_left(span, recv):
        remote(total.at[2, span, :], near_right.at[span, :], send_sem.at[16], recv, left).start()

    def reduce_near(g):
        lower, upper = halves(g)
        from_sibling(g, 1, x_right)
        total[1, upper, :] = pair_sum(x_right, upper).astype(BF16)
        to_right(upper, near_recv.at[g, 0])
        from_sibling(g, 2, x_left)
        total[2, lower, :] = pair_sum(x_left, lower).astype(BF16)
        to_left(lower, near_recv.at[g, 1])

    def reduce_3(g):
        half = pl.ds(g * HALF, HALF)
        lower, upper = halves(g)
        from_sibling(g, 1, x_right)
        arrived(far_left.at[half, :], far_recv.at[g, 0])
        total[1, lower, :] = (pair_sum(x_right, lower) + far_left[half, :].astype(F32)).astype(BF16)
        to_right(lower, near_recv.at[g, 2])
        from_sibling(g, 2, x_left)
        arrived(far_right.at[half, :], far_recv.at[g, 1])
        total[2, upper, :] = (pair_sum(x_left, upper) + far_right[half, :].astype(F32)).astype(BF16)
        to_left(upper, near_recv.at[g, 3])

    def slots(ref, d):
        return ref.at[pl.ds(pl.multiple_of(d * CAP, CAP), CAP), :]

    own_back = pltpu.make_async_copy(slots(back, 0), slots(table, 0), one_sem.at[5])

    def reduce_4(g):
        from_sibling(g, 3, x)
        lower, upper = halves(g)
        arrived(near_left.at[upper, :], near_recv.at[g, 0])
        arrived(near_right.at[lower, :], near_recv.at[g, 1])
        arrived(near_left.at[lower, :], near_recv.at[g, 2])
        arrived(near_right.at[upper, :], near_recv.at[g, 3])
        value = near_left[group(g), :].astype(F32) + near_right[group(g), :].astype(F32)
        back[group(g), :] = (pair_sum(x, group(g)) + value).astype(BF16)

        def give(d, carry):
            remote(slots(back, d), slots(table, d), send_sem.at[17], back_recv.at[g // 2], (back_to(d), h)).start()
            return carry

        if g == 0:
            own_back.start()
        lax.fori_loop(max(g * EG, 1), (g + 1) * EG, give, 0)

    def mix(p):
        lead = CAP if p == 0 else 0
        if p == 0:
            own_back.wait()
        arrived(table.at[pl.ds(p * PR + lead, PR - lead), :], back_recv.at[p])
        found, span = table[pl.ds(p * PR, PR), :], pl.ds(p * PR, PR)
        value = dot(weights[0, :, span], found) + dot(weights[1, :, span], found) + dot(weights[2, :, span], found)
        if p > 0:
            value = value + mixed[...]
        if p < NG // 2 - 1:
            mixed[...] = value
        else:
            dx_ref[...] = value.astype(BF16)

    run = dict(
        s1=gather_1, s2=gather_2, s3=gather_3, mid=expert_mid, near=reduce_near, mix=mix, out=expert_out, r2=reduce_2, r3=reduce_3, r4=reduce_4,
        within=within_block, weigh=weigh, scan=scan_states, finish=finish_states,
    )
    run["in"] = expert_in
    for name in order(NG, RANK):
        run[name[0]](*name[1:])

    ring, half_ring = rows.at[:, 0, :, 0:DC], rows.at[0, 0, :, 0:DC]
    for i, ref in (
        (0, out_rows.at[pl.ds(1, E - 1)]),
        (1, state_out.at[pl.ds(0, (E - 1) * SR), :]),
        (2, scan_out.at[pl.ds(0, (E - 1) * SR), :]),
        (3, ring), (4, ring), (5, half_ring), (6, half_ring),
        (7, ring), (8, ring), (9, ring), (10, half_ring), (11, half_ring),
        (12, part_in), (13, far_left), (14, far_right), (15, near_left), (16, near_right),
        (17, back.at[pl.ds(0, (E - 1) * CAP), :]),
    ):
        sent(ref, send_sem.at[i])


def copy_out(*refs):
    copies = [pltpu.make_async_copy(refs[i], refs[4 + i], refs[8].at[i]) for i in range(4)]
    for copy in copies:
        copy.start()
    for copy in copies:
        copy.wait()


def solution(mesh):
    E = mesh.shape["ctx"]
    NZ = min(8, E // 2)

    def shards(queries, keys, values, out_grad, log_decay, prefix_state, moe_input, moe_grad, gate, up, down, ids, probs):
        T, HL = queries.shape[0], log_decay.shape[0]
        DC, D, FL = moe_input.shape[1], gate.shape[1], gate.shape[2]
        gate, up, ids, probs = (jnp.swapaxes(array, -1, -2) for array in (gate, up, ids, probs))
        CAP = 4 * T // E
        NG = min(4, E // 2)
        ROWS, NR = E * CAP, E * CAP // NG
        vmem = pl.BlockSpec(memory_space=pltpu.VMEM)
        hbm = pl.BlockSpec(memory_space=pltpu.HBM)
        size = (E, E // NZ, NZ, T, CAP, DC, HL, NG)
        dma = pltpu.SemaphoreType.DMA
        results = [jax.ShapeDtypeStruct((T, HL * LANES), BF16)] * 3 + [jax.ShapeDtypeStruct((T, DC), BF16)]
        small = (
            ids, moe_input, moe_grad, log_decay, keys, values, queries, out_grad,
            prefix_state.reshape(HL * LANES, LANES), probs,
        )
        made = pl.pallas_call(
            functools.partial(kernel, size),
            out_shape=results,
            in_specs=[hbm] * 13,
            out_specs=[vmem] * 4,
            scratch_shapes=[pltpu.VMEM(array.shape, array.dtype) for array in small]
            + [
                pltpu.VMEM((FL, D), BF16),
                pltpu.VMEM((FL, D), BF16),
                pltpu.VMEM((FL, D), BF16),
                pltpu.VMEM((E, 2, CAP, DC), BF16),
                pltpu.VMEM((2, NX, ROWS, 2 * DC), BF16),
                pltpu.VMEM((NG // 2, 2 * NR, FL), F32),
                pltpu.VMEM((NG // 2, 2 * NR, FL), F32),
                pltpu.VMEM((NG // 2, 2 * NR, FL), F32),
                pltpu.VMEM((NG // 2, 2 * NR, FL), BF16),
                pltpu.VMEM((NG // 2, 2 * NR, FL), BF16),
                pltpu.VMEM((T, DC), F32),
                pltpu.VMEM((NX, ROWS, 2 * DC), BF16),
                pltpu.VMEM((NX, ROWS, DC), BF16),
                pltpu.VMEM((3, ROWS, DC), BF16),
                pltpu.VMEM((ROWS // 2, DC), BF16),
                pltpu.VMEM((ROWS // 2, DC), BF16),
                pltpu.VMEM((ROWS, DC), BF16),
                pltpu.VMEM((ROWS, DC), BF16),
                pltpu.VMEM((ROWS, DC), BF16),
                pltpu.VMEM((ROWS, DC), BF16),
                pltpu.VMEM((3, T, ROWS), BF16),
                pltpu.VMEM((HL * LANES, 3 * LANES), BF16),
                pltpu.VMEM((HL * LANES, 3 * LANES), BF16),
                pltpu.VMEM((HL * LANES, 2 * LANES), BF16),
                pltpu.VMEM((HL * LANES, 2 * LANES), BF16),
                pltpu.VMEM((3, T, HL * LANES), F32),
                pltpu.VMEM((HL, T, LANES), F32),
                pltpu.VMEM((HL, T, LANES), F32),
                dma((13,)),
                dma((6,)),
                dma((NG,)),
                dma((NG, 4)),
                dma((NG, 5)),
                dma((18,)),
                dma((NG // 2, 4)),
                dma((NG, 2)),
                dma((NG, 4)),
                dma((NG // 2,)),
            ],
            compiler_params=pltpu.CompilerParams(
                collective_id=0, has_side_effects=True, vmem_limit_bytes=52 * 1024 * 1024
            ),
        )(*(pltpu.with_memory_space_constraint(array, pltpu.HBM) for array in (*small, gate, up, down)))
        return pl.pallas_call(
            copy_out,
            out_shape=results,
            in_specs=[vmem] * 4,
            out_specs=[hbm] * 4,
            scratch_shapes=[dma((4,))],
        )(*(pltpu.with_memory_space_constraint(array, pltpu.VMEM) for array in made))

    in_specs = (
        P("ctx", "head"),
        P("ctx", "head"),
        P("ctx", "head"),
        P("ctx", "head"),
        P("head", "ctx"),
        P("head", None, None),
        P("ctx", "head"),
        P("ctx", "head"),
        P("ctx", None, "head"),
        P("ctx", None, "head"),
        P("ctx", "head", None),
        P("ctx", None),
        P("ctx", None),
    )
    out_specs = (P("ctx", "head"), P("ctx", "head"), P("ctx", "head"), P("ctx", "head"))
    return jax.shard_map(shards, mesh=mesh, in_specs=in_specs, out_specs=out_specs, check_vma=False)
```
